32 devices in a mesh: seg: 4 (over y, core), op: 8 (over z, x).
Axes of the slice: x: 2, y: 2, z: 4, core: 2. Of those that a mesh axis runs over, the one named last changes fastest.
Arguments:
- left_ops: float32 [4, 8, 768, 768], P('seg', 'op'), as said below
- right_ops: float32 [4, 8, 768, 768], P('seg', 'op'), as said below
- wavefunction: float32 [4, 768, 768], P('seg', 'op'), as said below
- basis_rotation: float32 [4, 768, 768], P('seg'), may hold values from -0.21875 to 0.21875
- pair_term: int32 [4, 8], P('seg', 'op'), may hold values from 0 to 15
- coupling: float32 [16], replicated, may hold values from 0.1 to 1
- left_charge: int32 [4, 768], P('seg'), may hold values from 0 to 2, as said below
- right_charge: int32 [4, 768], P('seg'), may hold values from 0 to 2, as said below
Outputs:
- chebyshev: float32 [4, 768, 768], P('seg', 'op')
- energy: float32 [4], P('seg')
- handed: float32 [4, 8, 768, 768], P('seg', 'op')
The draws below stay inside these ranges and needn't reach their ends.
Inputs may be any that keep to these rules, and one draw needn't show every extreme that they name: `left_ops`: each operator is a dominant positive diagonal plus dense full-rank off-diagonal entries. `right_ops`: each operator is a dominant positive diagonal plus dense full-rank off-diagonal entries. `wavefunction`: dense real entries of varying scale. `left_charge`: in each segment exactly 256 left bond states carry each quantum number. `right_charge`: in each segment exactly 256 right bond states carry each quantum number.
All inputs are finite; a program needn't handle non-finite values.
Results may differ from the reference program's by a relative error of at most 0.0003.
Values sent between devices are 32-bit elements; how exact they have to be, the bound alone decides.
No kernel may reach another device: no remote copies, remote signals or barrier semaphores. Data moves between devices by JAX's collectives and lax.ppermute only.
A program may use at most 128 MiB of HBM per device.

```python
import math
import jax
import jax.numpy as jnp
from jax import lax

M = 768
NTERMS = 16
NQ = 3
PAIRS = 8
SEGS = 4


def operator_stack(key):
    first_key, second_key = jax.random.split(key)
    scatter_part = jax.random.normal(first_key, (SEGS, PAIRS, M, M), jnp.float32) * M ** (-0.5)
    diagonal = jnp.exp(jax.random.uniform(second_key, (SEGS, PAIRS, 1, M), jnp.float32, 0.0, math.log(2.0)))
    identity = jnp.eye(M, dtype=jnp.float32)
    return scatter_part + identity * diagonal


def draw_left_ops(key, part):
    return operator_stack(jax.random.fold_in(key, 101))


def draw_right_ops(key, part):
    return operator_stack(jax.random.fold_in(key, 202))


def draw_wavefunction(key, part):
    base_key = jax.random.fold_in(key, 303)
    first_key, second_key, third_key = jax.random.split(base_key, 3)
    values = jax.random.normal(first_key, (SEGS, M, M), jnp.float32)
    rising = 3.0 ** (jnp.arange(M, dtype=jnp.float32) / M)
    row_scale = jnp.exp(jax.random.uniform(second_key, (SEGS, M, 1), jnp.float32, 0.0, math.log(10.0))) * rising[None, :, None]
    column_scale = jnp.exp(jax.random.uniform(third_key, (SEGS, 1, M), jnp.float32, 0.0, math.log(10.0)))
    return values * row_scale * column_scale


def balanced_charges(key):
    pattern = jnp.arange(M, dtype=jnp.int32) % NQ
    keys = jax.random.split(key, SEGS)
    return jax.vmap(lambda k: jax.random.permutation(k, pattern))(keys).astype(jnp.int32)


def draw_left_charge(key, part):
    return balanced_charges(jax.random.fold_in(key, 404))


def draw_right_charge(key, part):
    return balanced_charges(jax.random.fold_in(key, 505))


def touch_ends(result, stream_key, low, high):
    place = [jax.random.randint(jax.random.fold_in(stream_key, axis), (), 0, length) for axis, length in enumerate(result.shape)]
    main_axis = result.shape.index(max(result.shape))
    neighbour = place[:main_axis] + [(place[main_axis] + 1) % result.shape[main_axis]] + place[main_axis + 1:]
    return result.at[tuple(place)].set(low).at[tuple(neighbour)].set(high)


def block_scale(own_key, extent, cuts, least, largest):
    def one(position, shards_of):
        steps = jax.random.uniform(jax.random.fold_in(jax.random.fold_in(own_key, 6), position), (shards_of,), jnp.float32, least / len(cuts), largest / len(cuts))
        return jnp.repeat(jnp.exp(steps), extent[position] // shards_of).reshape((-1,) + (1,) * (len(extent) - position - 1))

    gain = one(*cuts[0])
    for cut in cuts[1:]:
        gain = gain * one(*cut)
    return gain


def bell_draw(key, extent, deviation, reach, shards=(), kind=jnp.bfloat16):
    entries = deviation * jax.random.normal(key, extent, jnp.float32)
    if shards:
        entries = entries * block_scale(key, extent, shards, -0.22, 0.18)
    return jnp.clip(entries, -reach, reach).astype(kind)


def setup_inputs(seed: int = 0) -> dict:
    splits = jax.random.split(jax.random.key(seed), 9)
    left_ops = draw_left_ops(jax.random.fold_in(splits[8], 71), 0)
    right_ops = draw_right_ops(jax.random.fold_in(splits[8], 71), 0)
    wavefunction = draw_wavefunction(jax.random.fold_in(splits[8], 71), 0)
    basis_rotation = bell_draw(splits[3], (SEGS, M, M), M ** -0.5, 0.21875, ((0, 4),), jnp.float32)
    pair_term = touch_ends(jax.random.randint(splits[4], (SEGS, PAIRS), 0, NTERMS), jax.random.fold_in(splits[4], 1), 0, NTERMS - 1).astype(jnp.int32)
    coupling = jnp.clip(jnp.exp(jax.random.uniform(splits[5], (NTERMS,), jnp.float32, math.log(0.1), math.log(1.0))), 0.1, 1.0)
    left_charge = draw_left_charge(jax.random.fold_in(splits[8], 71), 0)
    right_charge = draw_right_charge(jax.random.fold_in(splits[8], 71), 0)
    return {"left_ops": left_ops, "right_ops": right_ops, "wavefunction": wavefunction, "basis_rotation": basis_rotation, "pair_term": pair_term, "coupling": coupling, "left_charge": left_charge, "right_charge": right_charge}


HIGH = lax.Precision.HIGHEST

def apply_operator(vector, left_ops, right_ops, coefficient, sector_mask):
    partial_value = jnp.einsum('kab,bc->kac', left_ops, vector, precision=HIGH)
    partial_value = partial_value * coefficient[:, None, None]
    total = jnp.einsum('kac,kcd->ad', partial_value, right_ops, precision=HIGH)
    return total * sector_mask

def one_segment(items):
    left_ops, right_ops, wavefunction, basis_rotation, pair_term, coupling, left_charge, right_charge = items
    sector_mask = (left_charge[:, None] == right_charge[None, :]).astype(jnp.float32)
    coefficient = coupling[pair_term]
    width = float(M * M)
    masked = sector_mask * wavefunction
    initial = masked / jnp.sqrt(jnp.sum(masked * masked) / width + 1e-06)
    image_one = apply_operator(initial, left_ops, right_ops, coefficient, sector_mask)
    energy = jnp.sum(initial * image_one) / width
    spread = jnp.sqrt(jnp.sum(image_one * image_one) / width + 1e-06)
    first_step = (image_one - energy * initial) / spread
    image_two = apply_operator(first_step, left_ops, right_ops, coefficient, sector_mask)
    chebyshev = 2.0 * (image_two - energy * first_step) / spread - initial
    half_turn = jnp.einsum('kab,bj->kaj', left_ops, basis_rotation, precision=HIGH)
    rotated = jnp.einsum('ai,kaj->kij', basis_rotation, half_turn, precision=HIGH)
    return (chebyshev, energy, rotated)

def reference(left_ops, right_ops, wavefunction, basis_rotation, pair_term, coupling, left_charge, right_charge):
    copies = jnp.broadcast_to(coupling[None, :], (left_ops.shape[0], coupling.shape[0]))
    chebyshev, energy, rotated = lax.map(one_segment, (left_ops, right_ops, wavefunction, basis_rotation, pair_term, copies, left_charge, right_charge))
    handed = jnp.concatenate([left_ops[0:1], rotated[:-1]], axis=0)
    return (chebyshev, energy, handed)
```

```python
import functools

import jax
import jax.numpy as jnp
from jax import lax
from jax.experimental import pallas as pl
from jax.experimental.pallas import tpu as pltpu
from jax.sharding import PartitionSpec as P

NQ = 3
F32 = jnp.float32
BF16 = jnp.bfloat16
LANES = 128


VMEM = pl.BlockSpec(memory_space=pltpu.VMEM)
SMEM = pl.BlockSpec(memory_space=pltpu.SMEM)
LIMIT = pltpu.CompilerParams(vmem_limit_bytes=56 << 20)


def mm(a, b):
    return lax.dot_general(a, b, (((1,), (0,)), ((), ())), preferred_element_type=F32)


def mm_nt(a, b):
    return lax.dot_general(a, b, (((1,), (1,)), ((), ())), preferred_element_type=F32)


def split(x):
    high = x.astype(BF16)
    return high, (x - high.astype(F32)).astype(BF16)


def mm3(ah, al, bh, bl):
    return mm(ah, bh) + (mm(ah, bl) + mm(al, bh))


def places_of(charge, block):
    size = charge.shape[1]
    sector = lax.broadcasted_iota(jnp.int32, (16, size), 0)
    own = sector == charge
    earlier = lax.broadcasted_iota(jnp.int32, (size, size), 0) < lax.broadcasted_iota(jnp.int32, (size, size), 1)
    counts = mm(own.astype(F32).astype(BF16), earlier.astype(F32).astype(BF16))
    rank = jnp.sum(jnp.where(own, counts, 0.0), axis=0, keepdims=True)
    return rank + (charge * block).astype(F32)


def one_hot(places, positions):
    return (places == positions.astype(F32)).astype(F32).astype(BF16)


def sorter(place_row):
    size = place_row.shape[1]
    return one_hot(place_row, lax.broadcasted_iota(jnp.int32, (size, size), 0))


def column(row):
    return jnp.transpose(jnp.broadcast_to(row, (LANES, row.shape[1])))


def unsorter(place_column, size):
    return one_hot(place_column[:, :1], lax.broadcasted_iota(jnp.int32, (place_column.shape[0], size), 1))


def pack_kernel(me_ref, left_ref, right_ref, wave_ref, packed_ref, column_ref):
    rows, size = wave_ref.shape
    block = size // NQ
    place = places_of(right_ref[...], block)
    onto = sorter(place)
    column_ref[...] = column(left_ref[...].astype(F32))
    start = pl.multiple_of(me_ref[0] * rows, 8)
    charge = column_ref[pl.ds(start, rows), :][:, :1]
    wave = wave_ref[...]
    first, rest = split(wave)
    second, third = split(wave - first.astype(F32))
    ordered = mm_nt(first, onto) + (mm_nt(second, onto) + mm_nt(third, onto))
    packed = jnp.zeros((rows, block), F32)
    for q in range(NQ):
        packed = packed + jnp.where(charge == float(q), ordered[:, q * block : (q + 1) * block], 0.0)
    packed_ref[...] = packed


def sort_kernel(charge_ref, ops_ref, high_ref, low_ref, place_ref, onto, back, half_high, half_low):
    size = ops_ref.shape[1]
    rows = ops_ref.shape[0]
    step = pl.program_id(0)

    @pl.when(step == 0)
    def _():
        place = places_of(charge_ref[...], size // NQ)
        place_ref[...] = jnp.broadcast_to(place, place_ref.shape)
        onto[...] = sorter(place)
        back[...] = unsorter(column(place), size)

    high, low = split(ops_ref[...])
    start = pl.multiple_of(step * rows, rows)
    half_high[pl.ds(start, rows), :] = mm(high, back[...]).astype(BF16)
    half_low[pl.ds(start, rows), :] = mm(low, back[...]).astype(BF16)

    @pl.when(step == pl.num_programs(0) - 1)
    def _():
        for q in range(NQ):
            here = slice(q * (size // NQ), (q + 1) * (size // NQ))
            high_ref[here, :] = mm(onto[here, :], half_high[...]).astype(BF16)
            low_ref[here, :] = mm(onto[here, :], half_low[...]).astype(BF16)


def sorted_pieces(charge, ops):
    size = ops.shape[0]
    rows = size // NQ
    whole = lambda i: (0, 0)
    return pl.pallas_call(
        sort_kernel,
        grid=(NQ,),
        in_specs=[pl.BlockSpec((1, size), whole), pl.BlockSpec((rows, size), lambda i: (i, 0))],
        out_specs=[pl.BlockSpec((size, size), whole), pl.BlockSpec((size, size), whole), pl.BlockSpec((8, size), whole)],
        out_shape=[
            jax.ShapeDtypeStruct((size, size), BF16),
            jax.ShapeDtypeStruct((size, size), BF16),
            jax.ShapeDtypeStruct((8, size), F32),
        ],
        scratch_shapes=[pltpu.VMEM((size, size), BF16) for _ in range(4)],
        compiler_params=LIMIT,
    )(charge, ops)


def apply_blocks(packed, scale, left_high, left_low, right_high, right_low, half_high, half_low, total):
    block = packed.shape[1]
    for q in range(NQ):
        here = slice(q * block, (q + 1) * block)
        high, low = split(packed[here, :])
        value = mm3(left_high[:, here], left_low[:, here], high, low) * scale
        half_high[:, here], half_low[:, here] = split(value)
    for q in range(NQ):
        here = slice(q * block, (q + 1) * block)
        total[here, :] = mm3(half_high[here, :], half_low[here, :], right_high[:, here], right_low[:, here])


def first_kernel(count, me_ref, term_ref, table_ref, place_ref, *refs):
    parts = refs[:count]
    left_high, left_low, right_high, right_low = refs[count : count + 4]
    initial_ref = refs[count + 4]
    outs = refs[count + 5 : 2 * count + 5]
    half_high, half_low, total = refs[2 * count + 5 :]
    me = me_ref[0]
    rows, block = parts[0].shape
    size = rows * count
    for s in range(count):
        start = pl.multiple_of(lax.rem(me + (count - s), count) * rows, 8)
        total[pl.ds(start, rows), :] = parts[s][...]
    high, low = split(total[...])
    onto = sorter(place_ref[...][:1, :])
    packed = mm(onto, high) + mm(onto, low)
    norm = jnp.sqrt(jnp.sum(packed * packed, keepdims=True) / float(size * size) + 1e-06)
    initial = packed / norm
    initial_ref[...] = initial
    scale = table_ref[term_ref[0, 0]]
    apply_blocks(
        initial, scale, left_high, left_low, right_high, right_low, half_high, half_low, total
    )
    each = block // count
    for s in range(count):
        owner = lax.rem(me + s, count)
        for q in range(NQ):
            start = pl.multiple_of(q * block + owner * each, 8)
            outs[s][q * each : (q + 1) * each, :] = total[pl.ds(start, each), :]


def second_kernel(count, me_ref, term_ref, table_ref, place_ref, *refs):
    parts = refs[:count]
    initial_ref, left_high, left_low, right_high, right_low = refs[count : count + 5]
    step_ref, energy_ref, spread_ref = refs[count + 5 : count + 8]
    outs = refs[count + 8 : 2 * count + 8]
    half_high, half_low, total = refs[2 * count + 8 :]
    me = me_ref[0]
    rows, block = parts[0].shape
    size = rows * count
    each = block // count
    for s in range(count):
        owner = lax.rem(me + (count - s), count)
        for q in range(NQ):
            start = pl.multiple_of(q * block + owner * each, 8)
            total[pl.ds(start, each), :] = parts[s][q * each : (q + 1) * each, :]
    image = total[...]
    initial = initial_ref[...]
    width = float(size * size)
    energy = jnp.sum(initial * image, keepdims=True) / width
    spread = jnp.sqrt(jnp.sum(image * image, keepdims=True) / width + 1e-06)
    step = (image - energy * initial) / spread
    step_ref[...] = step
    energy_ref[...] = energy
    spread_ref[...] = spread
    scale = table_ref[term_ref[0, 0]]
    apply_blocks(step, scale, left_high, left_low, right_high, right_low, half_high, half_low, total)
    high, low = split(total[...])
    back = unsorter(column(place_ref[...][:1, :]), size)
    total[...] = mm(back, high) + mm(back, low)
    for s in range(count):
        start = pl.multiple_of(lax.rem(me + s, count) * rows, 8)
        outs[s][...] = total[pl.ds(start, rows), :]


def own_rows_kernel(me_ref, place_ref, initial_ref, step_ref, initial_rows_ref, step_rows_ref, column_ref):
    rows = initial_rows_ref.shape[0]
    size = initial_ref.shape[0]
    column_ref[...] = column(place_ref[...][:1, :])
    start = pl.multiple_of(me_ref[0] * rows, 8)
    back = unsorter(column_ref[pl.ds(start, rows), :], size)
    for source, target in ((initial_ref, initial_rows_ref), (step_ref, step_rows_ref)):
        high, low = split(source[...])
        target[...] = mm(back, high) + mm(back, low)


def last_kernel(count, me_ref, left_ref, place_ref, energy_ref, spread_ref, initial_ref, step_ref, *refs):
    parts = refs[:count]
    out_ref, column_ref = refs[count:]
    image = parts[0][...]
    for s in range(1, count):
        image = image + parts[s][...]
    rows, block = image.shape
    packed = 2.0 * (image - energy_ref[...] * step_ref[...]) / spread_ref[...] - initial_ref[...]
    column_ref[...] = column(left_ref[...].astype(F32))
    start = pl.multiple_of(me_ref[0] * rows, 8)
    charge = column_ref[pl.ds(start, rows), :][:, :1]
    onto = sorter(place_ref[...][:1, :])
    first, rest = split(packed)
    second, third = split(packed - first.astype(F32))
    out = jnp.zeros(out_ref.shape, F32)
    for piece in (first, second, third):
        wide = jnp.concatenate([jnp.where(charge == float(q), piece.astype(F32), 0.0) for q in range(NQ)], axis=1)
        out = out + mm(wide.astype(BF16), onto)
    out_ref[...] = out


def passed_along(value, axis, steps):
    count = lax.axis_size(axis)
    first, last = (max(0, -steps), min(count, count - steps))
    return lax.ppermute(value, axis, [(source, source + steps) for source in range(first, last)])


def turned(value, axis, steps):
    count = lax.axis_size(axis)
    return lax.ppermute(value, axis, [(source, (source + steps) % count) for source in range(count)])


def call(kernel, ins, shapes, scratch, *operands):
    return pl.pallas_call(
        kernel,
        in_specs=ins,
        out_specs=[VMEM] * len(shapes),
        out_shape=[jax.ShapeDtypeStruct(s, F32) for s in shapes],
        scratch_shapes=scratch,
        compiler_params=LIMIT,
    )(*operands)


def per_device(
    left_ops,
    right_ops,
    wavefunction,
    basis_rotation,
    pair_term,
    coupling,
    left_charge,
    right_charge,
):
    own_left = left_ops[0, 0]
    own_right = right_ops[0, 0]
    rows, size = wavefunction.shape[1:]
    block = size // NQ
    count = lax.axis_size("op")
    me = jnp.reshape(lax.axis_index("op").astype(jnp.int32), (1,))

    (packed,) = call(
        pack_kernel,
        [SMEM, VMEM, VMEM, VMEM],
        [(rows, block)],
        [pltpu.VMEM((size, LANES), F32)],
        me,
        left_charge,
        right_charge,
        wavefunction[0],
    )
    gathered = [packed] + [turned(packed, "op", s) for s in range(1, count)]

    left_high, left_low, left_place = sorted_pieces(left_charge, own_left)
    right_high, right_low, right_place = sorted_pieces(right_charge, own_right)
    pieces = (left_high, left_low, right_high, right_low)
    halves = [pltpu.VMEM((size, size), BF16), pltpu.VMEM((size, size), BF16), pltpu.VMEM((size, block), F32)]

    initial, *sent = call(
        functools.partial(first_kernel, count),
        [SMEM, SMEM, SMEM] + [VMEM] * (count + 5),
        [(size, block)] + [(rows, block)] * count,
        halves,
        me,
        pair_term,
        coupling,
        left_place,
        *gathered,
        *pieces,
    )
    own_sum = sent[0]
    for s in range(1, count):
        own_sum = own_sum + turned(sent[s], "op", s)
    gathered = [own_sum] + [turned(own_sum, "op", s) for s in range(1, count)]

    step, energy, spread, *sent = call(
        functools.partial(second_kernel, count),
        [SMEM, SMEM, SMEM] + [VMEM] * (count + 6),
        [(size, block), (1, 1), (1, 1)] + [(rows, block)] * count,
        halves,
        me,
        pair_term,
        coupling,
        left_place,
        *gathered,
        initial,
        *pieces,
    )
    received = [sent[0]] + [turned(sent[s], "op", s) for s in range(1, count)]
    initial_rows, step_rows = call(
        own_rows_kernel,
        [SMEM] + [VMEM] * 3,
        [(rows, block)] * 2,
        [pltpu.VMEM((size, LANES), F32)],
        me,
        left_place,
        initial,
        step,
    )
    (chebyshev,) = call(
        functools.partial(last_kernel, count),
        [SMEM] + [VMEM] * (count + 6),
        [(rows, size)],
        [pltpu.VMEM((size, LANES), F32)],
        me,
        left_charge,
        right_place,
        energy,
        spread,
        initial_rows,
        step_rows,
        *received,
    )

    half_turn = jnp.dot(own_left, basis_rotation[0], precision=lax.Precision.HIGH)
    rotated = lax.dot_general(
        basis_rotation[0], half_turn, (((0,), (0,)), ((), ())), precision=lax.Precision.HIGH
    )
    shifted = passed_along(rotated, "seg", 1)
    handed = jnp.where(lax.axis_index("seg") == 0, own_left, shifted)
    return (chebyshev[None], jnp.reshape(energy, (1,)), handed[None, None])


def solution(mesh):
    placed = (
        P("seg", "op", None, None),
        P("seg", "op", None, None),
        P("seg", "op", None),
        P("seg", None, None),
        P("seg", "op"),
        P(),
        P("seg", None),
        P("seg", None),
    )
    return jax.shard_map(
        per_device,
        mesh=mesh,
        in_specs=placed,
        out_specs=(P("seg", "op", None), P("seg"), P("seg", "op", None, None)),
        check_vma=False,
    )
```

```python
import functools

import jax
import jax.numpy as jnp
from jax import lax
from jax.experimental import pallas as pl
from jax.experimental.pallas import tpu as pltpu
from jax.sharding import PartitionSpec as P


NQ = 3
F32 = jnp.float32
BF16 = jnp.bfloat16
LANES = 128


VMEM = pl.BlockSpec(memory_space=pltpu.VMEM)
SMEM = pl.BlockSpec(memory_space=pltpu.SMEM)
HBM = pl.BlockSpec(memory_space=pltpu.HBM)
LIMIT = pltpu.CompilerParams(vmem_limit_bytes=16 << 20)
SMALL = pltpu.CompilerParams(vmem_limit_bytes=4 << 20)


def mm(a, b):
    return lax.dot_general(a, b, (((1,), (0,)), ((), ())), preferred_element_type=F32)


def split(x):
    high = x.astype(BF16)
    return high, (x - high.astype(F32)).astype(BF16)


def mm3(ah, al, bh, bl):
    return mm(ah, bh) + (mm(ah, bl) + mm(al, bh))


def places_of(charge, block):
    size = charge.shape[1]
    own = (lax.broadcasted_iota(jnp.int32, (16, size), 0) == charge).astype(F32)
    earlier = lax.broadcasted_iota(jnp.int32, (LANES, LANES), 0) < lax.broadcasted_iota(jnp.int32, (LANES, LANES), 1)
    earlier = earlier.astype(F32).astype(BF16)
    before = jnp.zeros((16, 1), F32)
    ranks = []
    for c in range(size // LANES):
        part = own[:, c * LANES : (c + 1) * LANES]
        counts = mm(part.astype(BF16), earlier) + before
        ranks.append(jnp.sum(part * counts, axis=0, keepdims=True))
        before = before + jnp.sum(part, axis=1, keepdims=True)
    return jnp.concatenate(ranks, axis=1) + (charge * block).astype(F32)


def chosen(places, positions):
    return jnp.where(places.astype(BF16) == positions, jnp.ones((), BF16), jnp.zeros((), BF16))


def sorter(place_row):
    size = place_row.shape[1]
    step = 2 * LANES
    place = lax.broadcasted_iota(jnp.int32, (step, size), 0).astype(F32).astype(BF16)
    row = jnp.broadcast_to(place_row, (step, size))
    return jnp.concatenate([chosen(row - float(c), place) for c in range(0, size, step)], axis=0)


def column(row):
    return jnp.transpose(jnp.broadcast_to(row, (LANES, row.shape[1])))


def unsorter(place_column, size):
    lane = lax.broadcasted_iota(jnp.int32, place_column.shape, 1).astype(F32).astype(BF16)
    return jnp.concatenate([chosen(place_column - float(c), lane) for c in range(0, size, LANES)], axis=1)


def pack_kernel(
    me_ref, left_hbm, right_hbm, wave_hbm, packed_ref, column_ref, left_ref, right_ref, wave_ref, arrived
):
    rows, size = wave_ref.shape
    block = size // NQ
    copies = [
        pltpu.make_async_copy(source, target, arrived.at[i])
        for i, (source, target) in enumerate(
            ((right_hbm, right_ref), (left_hbm, left_ref), (wave_hbm, wave_ref))
        )
    ]
    for copy in copies:
        copy.start()
    for copy in copies:
        copy.wait()
    back = unsorter(column(places_of(right_ref[...], block)), size)
    column_ref[...] = column(left_ref[...].astype(F32))
    start = pl.multiple_of(me_ref[0] * rows, 8)
    charge = column_ref[pl.ds(start, rows), :][:, :1]
    wave = wave_ref[...]
    first, _ = split(wave)
    second, third = split(wave - first.astype(F32))
    ordered = mm(first, back) + (mm(second, back) + mm(third, back))
    packed = jnp.zeros((rows, block), F32)
    for q in range(NQ):
        packed = packed + jnp.where(charge == float(q), ordered[:, q * block : (q + 1) * block], 0.0)
    packed_ref[...] = packed


def columns_kernel(charge_ref, ops_ref, half_high, half_low, onto, back, column_ref):
    rows, size = ops_ref.shape
    step = pl.program_id(0)

    @pl.when(step == 0)
    def _():
        place = places_of(charge_ref[...], size // NQ)
        column_ref[...] = column(place)
        onto[...] = sorter(place)
        back[...] = unsorter(column_ref[...], size)

    high, low = split(ops_ref[...])
    here = pl.ds(pl.multiple_of(step * rows, rows), rows)
    half_high[here, :] = mm(high, back[...]).astype(BF16)
    half_low[here, :] = mm(low, back[...]).astype(BF16)


def sort_kernel(
    charge_ref,
    left_half_high,
    left_half_low,
    left_onto,
    ops_ref,
    left_high,
    left_low,
    right_high,
    right_low,
    place_ref,
    onto,
    back,
    half_high,
    half_low,
):
    rows, size = ops_ref.shape
    step = pl.program_id(0)

    @pl.when(step == 0)
    def _():
        place = places_of(charge_ref[...], size // NQ)
        place_ref[...] = jnp.broadcast_to(place, place_ref.shape)
        onto[...] = sorter(place)
        back[...] = unsorter(column(place), size)

    here = pl.ds(pl.multiple_of(step * rows, rows), rows)
    left_high[here, :] = mm(left_onto[here, :], left_half_high[...]).astype(BF16)
    left_low[here, :] = mm(left_onto[here, :], left_half_low[...]).astype(BF16)
    high, low = split(ops_ref[...])
    half_high[here, :] = mm(high, back[...]).astype(BF16)
    half_low[here, :] = mm(low, back[...]).astype(BF16)

    @pl.when(step == pl.num_programs(0) - 1)
    def _():
        for q in range(NQ):
            there = slice(q * rows, (q + 1) * rows)
            right_high[there, :] = mm(onto[there, :], half_high[...]).astype(BF16)
            right_low[there, :] = mm(onto[there, :], half_low[...]).astype(BF16)


def sort_columns(charge, ops):
    size = ops.shape[0]
    rows = size // NQ
    return pl.pallas_call(
        columns_kernel,
        grid=(NQ,),
        in_specs=[VMEM, pl.BlockSpec((rows, size), lambda i: (i, 0))],
        out_specs=[VMEM] * 5,
        out_shape=[pltpu.VMEM((size, size), BF16)] * 4 + [pltpu.VMEM((size, LANES), F32)],
        compiler_params=LIMIT,
    )(far(charge), far(ops))


def sort_rest(charge, left_half_high, left_half_low, left_onto, ops):
    size = ops.shape[0]
    rows = size // NQ
    return pl.pallas_call(
        sort_kernel,
        grid=(NQ,),
        in_specs=[VMEM] * 4 + [pl.BlockSpec((rows, size), lambda i: (i, 0))],
        out_specs=[VMEM] * 5,
        out_shape=[pltpu.VMEM((size, size), BF16)] * 4 + [jax.ShapeDtypeStruct((8, size), F32)],
        scratch_shapes=[pltpu.VMEM((size, size), BF16) for _ in range(4)],
        compiler_params=LIMIT,
    )(far(charge), left_half_high, left_half_low, left_onto, far(ops))


def apply_blocks(packed, scale, left_high, left_low, right_high, right_low, half_high, half_low, total):
    block = packed.shape[1]
    for q in range(NQ):
        here = slice(q * block, (q + 1) * block)
        high, low = split(packed[here, :])
        value = mm3(left_high[:, here], left_low[:, here], high, low) * scale
        half_high[:, here], half_low[:, here] = split(value)
    for q in range(NQ):
        here = slice(q * block, (q + 1) * block)
        total[here, :] = mm3(half_high[here, :], half_low[here, :], right_high[:, here], right_low[:, here])


def first_kernel(group, me_ref, term_ref, table_ref, onto_ref, *refs):
    parts = refs[:group]
    left_high, left_low, right_high, right_low = refs[group : group + 4]
    initial_ref, initial_rows_ref = refs[group + 4 : group + 6]
    outs = refs[group + 6 : 2 * group + 6]
    half_high, half_low, total = refs[2 * group + 6 :]
    half = lax.div(me_ref[0], group)
    own = lax.rem(me_ref[0], group)
    pair, block = parts[0].shape
    rows = pair // 2
    size = pair * group
    for s in range(group):
        for h, side in enumerate((half, 1 - half)):
            start = pl.multiple_of((side * group + (own ^ s)) * rows, 8)
            total[pl.ds(start, rows), :] = parts[s][h * rows : (h + 1) * rows, :]
    high, low = split(total[...])
    packed = mm(onto_ref[...], high) + mm(onto_ref[...], low)
    norm = jnp.sqrt(jnp.sum(packed * packed, keepdims=True) / float(size * size) + 1e-06)
    initial_ref[...] = packed / norm
    initial_rows_ref[...] = parts[0][:rows, :] / norm
    scale = table_ref[term_ref[0, 0]]
    apply_blocks(
        initial_ref[...], scale, left_high, left_low, right_high, right_low, half_high, half_low, total
    )
    each = block // group
    for s in range(group):
        for q in range(NQ):
            start = pl.multiple_of(q * block + (own ^ s) * each, 8)
            outs[s][q * each : (q + 1) * each, :] = total[pl.ds(start, each), :]


def second_kernel(group, me_ref, term_ref, table_ref, back_ref, column_ref, *refs):
    parts = refs[:group]
    initial_ref, left_high, left_low, right_high, right_low = refs[group : group + 5]
    energy_ref, spread_ref, step_rows_ref, spot_ref = refs[group + 5 : group + 9]
    outs = refs[group + 9 : 2 * group + 9]
    half_high, half_low, total, step_ref = refs[2 * group + 9 :]
    half = lax.div(me_ref[0], group)
    own = lax.rem(me_ref[0], group)
    pair, block = parts[0].shape
    rows = pair // 2
    size = pair * group
    each = block // group
    for s in range(group):
        for q in range(NQ):
            start = pl.multiple_of(q * block + (own ^ s) * each, 8)
            total[pl.ds(start, each), :] = parts[s][q * each : (q + 1) * each, :]
    width = float(size * size)
    energy = jnp.sum(initial_ref[...] * total[...], keepdims=True) / width
    spread = jnp.sqrt(jnp.sum(total[...] * total[...], keepdims=True) / width + 1e-06)
    step_ref[...] = (total[...] - energy * initial_ref[...]) / spread
    energy_ref[...] = energy
    spread_ref[...] = spread
    scale = table_ref[term_ref[0, 0]]
    apply_blocks(
        step_ref[...], scale, left_high, left_low, right_high, right_low, half_high, half_low, total
    )
    high, low = split(total[...])
    total[...] = mm(back_ref[...], high) + mm(back_ref[...], low)
    start = pl.multiple_of(me_ref[0] * rows, 8)
    spot_ref[...] = column_ref[pl.ds(start, rows), :]
    back = unsorter(spot_ref[...], size)
    high, low = split(step_ref[...])
    step_rows_ref[...] = mm(back, high) + mm(back, low)
    for s in range(group):
        for h, side in enumerate((half, 1 - half)):
            start = pl.multiple_of((side * group + (own ^ s)) * rows, 8)
            outs[s][h * rows : (h + 1) * rows, :] = total[pl.ds(start, rows), :]


def last_kernel(spot_ref, place_ref, energy_ref, spread_ref, initial_ref, step_ref, kept_ref, sent_ref, out_ref):
    image = kept_ref[...] + sent_ref[...]
    packed = 2.0 * (image - energy_ref[...] * step_ref[...]) / spread_ref[...] - initial_ref[...]
    block = packed.shape[1]
    spot = jnp.broadcast_to(spot_ref[...][:, :1], packed.shape)
    held = [(spot >= float(q * block)) & (spot < float((q + 1) * block)) for q in range(NQ)]
    onto = sorter(place_ref[...][:1, :])
    high = packed.astype(BF16).astype(F32)
    out = jnp.zeros(out_ref.shape, F32)
    for piece in (high, packed - high):
        wide = jnp.concatenate([jnp.where(here, piece, 0.0) for here in held], axis=1)
        out = out + mm(wide.astype(BF16), onto)
    out_ref[...] = out


def join_kernel(first_ref, second_ref, out_ref):
    rows = first_ref.shape[0]
    out_ref[:rows, :] = first_ref[...]
    out_ref[rows:, :] = second_ref[...]


def sum_kernel(*refs):
    parts = [ref for ref in refs if ref.shape == refs[0].shape]
    outs = refs[len(parts) :]
    if not outs:
        parts, outs = parts[:-1], parts[-1:]
    start = 0
    for out in outs:
        here = slice(start, start + out.shape[0])
        start += out.shape[0]
        value = parts[0][here, :]
        for part in parts[1:]:
            value = value + part[here, :]
        out[...] = value


def choose_kernel(segment_ref, own_ref, shifted_ref, out_ref, held, arrived, left):
    rows = own_ref.shape[0] // NQ
    parts = [slice(q * rows, (q + 1) * rows) for q in range(NQ)]
    outs = [pltpu.make_async_copy(held.at[p], out_ref.at[p], left.at[q]) for q, p in enumerate(parts)]

    def through(source):
        ins = [pltpu.make_async_copy(source.at[p], held.at[p], arrived.at[q]) for q, p in enumerate(parts)]
        for copy in ins:
            copy.start()
        for come, go in zip(ins, outs):
            come.wait()
            go.start()

    pl.when(segment_ref[0] == 0)(lambda: through(own_ref))
    pl.when(segment_ref[0] != 0)(lambda: through(shifted_ref))
    for copy in outs:
        copy.wait()


def passed_along(value, axis, steps):
    count = lax.axis_size(axis)
    first, last = (max(0, -steps), min(count, count - steps))
    return lax.ppermute(value, axis, [(source, source + steps) for source in range(first, last)])


def near(value):
    return pltpu.with_memory_space_constraint(value, pltpu.VMEM)


def far(value):
    return pltpu.with_memory_space_constraint(value, pltpu.HBM)


def swapped(value, axis, mask):
    count = lax.axis_size(axis)
    return near(lax.ppermute(value, axis, [(source, source ^ mask) for source in range(count)]))


def call(kernel, ins, outs, scratch, *operands, params=SMALL):
    return pl.pallas_call(
        kernel,
        in_specs=ins,
        out_specs=[VMEM] * len(outs),
        out_shape=outs,
        scratch_shapes=scratch,
        compiler_params=params,
    )(*operands)


def summed(heights, *parts):
    outs = [pltpu.VMEM((h,) + parts[0].shape[1:], F32) for h in heights]
    return call(sum_kernel, [VMEM] * len(parts), outs, [], *parts)


def all_steps(
    left_ops,
    right_ops,
    wavefunction,
    basis_rotation,
    pair_term,
    coupling,
    left_charge,
    right_charge,
):
    own_left = left_ops[0, 0]
    own_right = right_ops[0, 0]
    rows, size = wavefunction.shape[1:]
    block = size // NQ
    count = lax.axis_size("op")
    group = count // 2
    me = jnp.reshape(lax.axis_index("op").astype(jnp.int32), (1,))

    (packed,) = call(
        pack_kernel,
        [SMEM, HBM, HBM, HBM],
        [pltpu.VMEM((rows, block), F32)],
        [
            pltpu.VMEM((size, LANES), F32),
            pltpu.VMEM((1, size), jnp.int32),
            pltpu.VMEM((1, size), jnp.int32),
            pltpu.VMEM((rows, size), F32),
            pltpu.SemaphoreType.DMA((3,)),
        ],
        me,
        far(left_charge),
        far(right_charge),
        far(wavefunction[0]),
    )
    (pair,) = call(
        join_kernel, [VMEM] * 2, [pltpu.VMEM((2 * rows, block), F32)], [], packed, swapped(packed, "op", group)
    )
    gathered = [pair] + [swapped(pair, "op", s) for s in range(1, group)]

    left_half_high, left_half_low, onto, back, left_column = sort_columns(left_charge, own_left)
    left_high, left_low, right_high, right_low, right_place = sort_rest(
        right_charge, left_half_high, left_half_low, onto, own_right
    )
    pieces = (left_high, left_low, right_high, right_low)
    halves = [pltpu.VMEM((size, size), BF16), pltpu.VMEM((size, size), BF16), pltpu.VMEM((size, block), F32)]
    pairs = [pltpu.VMEM((2 * rows, block), F32)] * group

    initial, initial_rows, *sent = call(
        functools.partial(first_kernel, group),
        [SMEM, SMEM, SMEM] + [VMEM] * (group + 5),
        [pltpu.VMEM((size, block), F32), pltpu.VMEM((rows, block), F32)] + pairs,
        halves,
        me,
        pair_term,
        coupling,
        onto,
        *gathered,
        *pieces,
        params=LIMIT,
    )
    total = summed([2 * rows], sent[0], *[swapped(sent[s], "op", s) for s in range(group - 1, 0, -1)])[0]
    total = summed([2 * rows], total, swapped(total, "op", group))[0]
    gathered = [total] + [swapped(total, "op", s) for s in range(group - 1, 0, -1)][::-1]

    energy, spread, step_rows, spot, *sent = call(
        functools.partial(second_kernel, group),
        [SMEM, SMEM, SMEM] + [VMEM] * (group + 7),
        [
            pltpu.VMEM((1, 1), F32),
            pltpu.VMEM((1, 1), F32),
            pltpu.VMEM((rows, block), F32),
            pltpu.VMEM((rows, LANES), F32),
        ]
        + pairs,
        halves + [pltpu.VMEM((size, block), F32)],
        me,
        pair_term,
        coupling,
        back,
        near(left_column),
        *gathered,
        initial,
        *pieces,
        params=LIMIT,
    )
    kept, away = summed([rows, rows], near(sent[0]), *[swapped(sent[s], "op", s) for s in range(group - 1, 0, -1)])
    received = swapped(away, "op", group)
    (chebyshev,) = call(
        last_kernel,
        [VMEM] * 8,
        [jax.ShapeDtypeStruct((rows, size), F32)],
        [],
        near(spot),
        right_place,
        near(energy),
        near(spread),
        near(initial_rows),
        near(step_rows),
        near(kept),
        received,
    )

    turned_left, _ = lax.optimization_barrier((own_left, initial))
    half_turn = jnp.dot(turned_left, basis_rotation[0], precision=lax.Precision.HIGH)
    rotated = lax.dot_general(
        basis_rotation[0], half_turn, (((0,), (0,)), ((), ())), precision=lax.Precision.HIGH
    )
    shifted = passed_along(far(rotated), "seg", 1)
    segment = jnp.reshape(lax.axis_index("seg").astype(jnp.int32), (1,))
    handed = pl.pallas_call(
        choose_kernel,
        in_specs=[SMEM, HBM, HBM],
        out_specs=HBM,
        out_shape=jax.ShapeDtypeStruct((size, size), F32),
        scratch_shapes=[pltpu.VMEM((size, size), F32), pltpu.SemaphoreType.DMA((NQ,)), pltpu.SemaphoreType.DMA((NQ,))],
        compiler_params=SMALL,
    )(segment, far(own_left), far(shifted))[None, None]
    return (chebyshev[None], energy[0], handed)


def solution(mesh):
    placed = (
        P("seg", "op", None, None),
        P("seg", "op", None, None),
        P("seg", "op", None),
        P("seg", None, None),
        P("seg", "op"),
        P(),
        P("seg", None),
        P("seg", None),
    )
    return jax.shard_map(
        all_steps,
        mesh=mesh,
        in_specs=placed,
        out_specs=(P("seg", "op", None), P("seg"), P("seg", "op", None, None)),
        check_vma=False,
    )
```

```python
import functools

import jax
import jax.numpy as jnp
from jax import lax
from jax.experimental import pallas as pl
from jax.experimental.pallas import tpu as pltpu
from jax.sharding import PartitionSpec as P


NQ = 3
F32 = jnp.float32
BF16 = jnp.bfloat16
LANES = 128


VMEM = pl.BlockSpec(memory_space=pltpu.VMEM)
SMEM = pl.BlockSpec(memory_space=pltpu.SMEM)
HBM = pl.BlockSpec(memory_space=pltpu.HBM)
LIMIT = pltpu.CompilerParams(vmem_limit_bytes=16 << 20)
SMALL = pltpu.CompilerParams(vmem_limit_bytes=4 << 20)


def mm(a, b):
    return lax.dot_general(a, b, (((1,), (0,)), ((), ())), preferred_element_type=F32)


def split(x):
    high = x.astype(BF16)
    return high, (x - high.astype(F32)).astype(BF16)


def mm3(ah, al, bh, bl):
    return mm(ah, bh) + (mm(ah, bl) + mm(al, bh))


def places_of(charge, block):
    size = charge.shape[1]
    own = (lax.broadcasted_iota(jnp.int32, (16, size), 0) == charge).astype(F32)
    earlier = lax.broadcasted_iota(jnp.int32, (LANES, LANES), 0) < lax.broadcasted_iota(jnp.int32, (LANES, LANES), 1)
    earlier = earlier.astype(F32).astype(BF16)
    before = jnp.zeros((16, 1), F32)
    ranks = []
    for c in range(size // LANES):
        part = own[:, c * LANES : (c + 1) * LANES]
        counts = mm(part.astype(BF16), earlier) + before
        ranks.append(jnp.sum(part * counts, axis=0, keepdims=True))
        before = before + jnp.sum(part, axis=1, keepdims=True)
    return jnp.concatenate(ranks, axis=1) + (charge * block).astype(F32)


def chosen(places, positions):
    return jnp.where(places.astype(BF16) == positions, jnp.ones((), BF16), jnp.zeros((), BF16))


def sorter(place_row):
    size = place_row.shape[1]
    step = 2 * LANES
    place = lax.broadcasted_iota(jnp.int32, (step, size), 0).astype(F32).astype(BF16)
    row = jnp.broadcast_to(place_row, (step, size))
    return jnp.concatenate([chosen(row - float(c), place) for c in range(0, size, step)], axis=0)


def column(row):
    return jnp.transpose(jnp.broadcast_to(row, (LANES, row.shape[1])))


def unsorter(place_column, size):
    lane = lax.broadcasted_iota(jnp.int32, place_column.shape, 1).astype(F32).astype(BF16)
    return jnp.concatenate([chosen(place_column - float(c), lane) for c in range(0, size, LANES)], axis=1)


def pack_kernel(
    me_ref, left_hbm, right_hbm, wave_hbm, packed_ref, column_ref, left_ref, right_ref, wave_ref, arrived
):
    rows, size = wave_ref.shape
    block = size // NQ
    copies = [
        pltpu.make_async_copy(source, target, arrived.at[i])
        for i, (source, target) in enumerate(
            ((right_hbm, right_ref), (left_hbm, left_ref), (wave_hbm, wave_ref))
        )
    ]
    for copy in copies:
        copy.start()
    copies[0].wait()
    back = unsorter(column(places_of(right_ref[...], block)), size)
    copies[1].wait()
    column_ref[...] = column(left_ref[...].astype(F32))
    start = pl.multiple_of(me_ref[0] * rows, 8)
    charge = column_ref[pl.ds(start, rows), :][:, :1]
    copies[2].wait()
    both = mm(jnp.concatenate(split(wave_ref[...]), axis=0), back)
    ordered = both[:rows, :] + both[rows:, :]
    packed = jnp.zeros((rows, block), F32)
    for q in range(NQ):
        packed = packed + jnp.where(charge == float(q), ordered[:, q * block : (q + 1) * block], 0.0)
    packed_ref[...] = packed


def columns_kernel(charge_ref, ops_ref, half_high, half_low, onto, back, column_ref):
    rows, size = ops_ref.shape
    step = pl.program_id(0)

    @pl.when(step == 0)
    def _():
        place = places_of(charge_ref[...], size // NQ)
        column_ref[...] = column(place)
        onto[...] = sorter(place)
        back[...] = unsorter(column_ref[...], size)

    high, low = split(ops_ref[...])
    here = pl.ds(pl.multiple_of(step * rows, rows), rows)
    half_high[here, :] = mm(high, back[...]).astype(BF16)
    half_low[here, :] = mm(low, back[...]).astype(BF16)


def sort_kernel(
    charge_ref,
    left_half_high,
    left_half_low,
    left_onto,
    ops_ref,
    left_high,
    left_low,
    right_high,
    right_low,
    onto,
    back,
    half_high,
    half_low,
):
    rows, size = ops_ref.shape
    step = pl.program_id(0)

    @pl.when(step == 0)
    def _():
        place = places_of(charge_ref[...], size // NQ)
        onto[...] = sorter(place)
        back[...] = unsorter(column(place), size)

    here = pl.ds(pl.multiple_of(step * rows, rows), rows)
    left_high[here, :] = mm(left_onto[here, :], left_half_high[...]).astype(BF16)
    left_low[here, :] = mm(left_onto[here, :], left_half_low[...]).astype(BF16)
    high, low = split(ops_ref[...])
    half_high[here, :] = mm(high, back[...]).astype(BF16)
    half_low[here, :] = mm(low, back[...]).astype(BF16)

    @pl.when(step == pl.num_programs(0) - 1)
    def _():
        for q in range(NQ):
            there = slice(q * rows, (q + 1) * rows)
            right_high[there, :] = mm(onto[there, :], half_high[...]).astype(BF16)
            right_low[there, :] = mm(onto[there, :], half_low[...]).astype(BF16)


def sort_columns(charge, ops):
    size = ops.shape[0]
    rows = size // NQ
    return pl.pallas_call(
        columns_kernel,
        grid=(NQ,),
        in_specs=[VMEM, pl.BlockSpec((rows, size), lambda i: (i, 0))],
        out_specs=[VMEM] * 5,
        out_shape=[pltpu.VMEM((size, size), BF16)] * 4 + [pltpu.VMEM((size, LANES), F32)],
        compiler_params=LIMIT,
    )(far(charge), far(ops))


def sort_rest(charge, left_half_high, left_half_low, left_onto, ops):
    size = ops.shape[0]
    rows = size // NQ
    return pl.pallas_call(
        sort_kernel,
        grid=(NQ,),
        in_specs=[VMEM] * 4 + [pl.BlockSpec((rows, size), lambda i: (i, 0))],
        out_specs=[VMEM] * 4,
        out_shape=[pltpu.VMEM((size, size), BF16)] * 4,
        scratch_shapes=[pltpu.VMEM((size, size), BF16) for _ in range(4)],
        compiler_params=LIMIT,
    )(far(charge), left_half_high, left_half_low, left_onto, far(ops))


def apply_blocks(packed, scale, left_high, left_low, right_high, right_low, half_high, half_low, total):
    block = packed.shape[1]
    for q in range(NQ):
        here = slice(q * block, (q + 1) * block)
        high, low = split(packed[here, :])
        value = mm3(left_high[:, here], left_low[:, here], high, low) * scale
        half_high[:, here], half_low[:, here] = split(value)
    for q in range(NQ):
        here = slice(q * block, (q + 1) * block)
        total[here, :] = mm3(half_high[here, :], half_low[here, :], right_high[:, here], right_low[:, here])


def first_kernel(group, me_ref, term_ref, table_ref, onto_ref, *refs):
    parts = refs[:group]
    left_high, left_low, right_high, right_low = refs[group : group + 4]
    initial_ref, initial_rows_ref = refs[group + 4 : group + 6]
    outs = refs[group + 6 : 2 * group + 6]
    half_high, half_low, total = refs[2 * group + 6 :]
    half = lax.div(me_ref[0], group)
    own = lax.rem(me_ref[0], group)
    pair, block = parts[0].shape
    rows = pair // 2
    size = pair * group
    for s in range(group):
        for h, side in enumerate((half, 1 - half)):
            start = pl.multiple_of((side * group + (own ^ s)) * rows, 8)
            total[pl.ds(start, rows), :] = parts[s][h * rows : (h + 1) * rows, :]
    high, low = split(total[...])
    packed = mm(onto_ref[...], high) + mm(onto_ref[...], low)
    norm = jnp.sqrt(jnp.sum(packed * packed, keepdims=True) / float(size * size) + 1e-06)
    initial_ref[...] = packed / norm
    initial_rows_ref[...] = parts[0][:rows, :] / norm
    scale = table_ref[term_ref[0, 0]]
    apply_blocks(
        initial_ref[...], scale, left_high, left_low, right_high, right_low, half_high, half_low, total
    )
    each = block // group
    for s in range(group):
        for q in range(NQ):
            start = pl.multiple_of(q * block + (own ^ s) * each, 8)
            outs[s][q * each : (q + 1) * each, :] = total[pl.ds(start, each), :]


def second_kernel(group, me_ref, term_ref, table_ref, back_ref, column_ref, *refs):
    count = 2 * group
    parts = refs[:count]
    initial_ref, left_high, left_low, right_high, right_low = refs[count : count + 5]
    energy_ref, spread_ref, step_rows_ref, spot_ref = refs[count + 5 : count + 9]
    outs = refs[count + 9 : 2 * count + 9]
    half_high, half_low, total, step_ref = refs[2 * count + 9 :]
    half = lax.div(me_ref[0], group)
    own = lax.rem(me_ref[0], group)
    pair, width = parts[0].shape
    block = 2 * width
    sides = [slice(c * width, (c + 1) * width) for c in range(2)]
    rows = pair // 2
    size = pair * group
    each = block // group
    for s in range(group):
        for q in range(NQ):
            start = pl.multiple_of(q * block + (own ^ s) * each, 8)
            for c in range(2):
                total[pl.ds(start, each), sides[c]] = parts[c * group + s][q * each : (q + 1) * each, :]
    cells = float(size * size)
    energy = jnp.sum(initial_ref[...] * total[...], keepdims=True) / cells
    spread = jnp.sqrt(jnp.sum(total[...] * total[...], keepdims=True) / cells + 1e-06)
    step_ref[...] = (total[...] - energy * initial_ref[...]) / spread
    energy_ref[...] = energy
    spread_ref[...] = spread
    scale = table_ref[term_ref[0, 0]]
    apply_blocks(
        step_ref[...], scale, left_high, left_low, right_high, right_low, half_high, half_low, total
    )
    high, low = split(total[...])
    total[...] = mm(back_ref[...], high) + mm(back_ref[...], low)
    start = pl.multiple_of(me_ref[0] * rows, 8)
    spot_ref[...] = column_ref[pl.ds(start, rows), :]
    back = unsorter(spot_ref[...], size)
    high, low = split(step_ref[...])
    step_rows_ref[...] = mm(back, high) + mm(back, low)
    for s in range(group):
        for h, side in enumerate((half, 1 - half)):
            start = pl.multiple_of((side * group + (own ^ s)) * rows, 8)
            for c in range(2):
                outs[c * group + s][h * rows : (h + 1) * rows, :] = total[pl.ds(start, rows), sides[c]]


def order_kernel(charge_ref, onto_ref):
    onto_ref[...] = sorter(places_of(charge_ref[...], charge_ref.shape[1] // NQ))


def last_kernel(spot_ref, onto_ref, energy_ref, spread_ref, initial_ref, step_ref, *refs):
    kept, sent, out_ref = refs[:2], refs[2:4], refs[4]
    image = jnp.concatenate([a[...] + b[...] for a, b in zip(kept, sent)], axis=1)
    packed = 2.0 * (image - energy_ref[...] * step_ref[...]) / spread_ref[...] - initial_ref[...]
    block = packed.shape[1]
    spot = jnp.broadcast_to(spot_ref[...][:, :1], packed.shape)
    held = [(spot >= float(q * block)) & (spot < float((q + 1) * block)) for q in range(NQ)]
    high = packed.astype(BF16).astype(F32)
    wide = [
        jnp.concatenate([jnp.where(here, piece, 0.0) for here in held], axis=1) for piece in (high, packed - high)
    ]
    both = mm(jnp.concatenate(wide, axis=0).astype(BF16), onto_ref[...])
    rows = packed.shape[0]
    out_ref[...] = both[:rows, :] + both[rows:, :]


def join_kernel(first_ref, second_ref, out_ref):
    rows = first_ref.shape[0]
    out_ref[:rows, :] = first_ref[...]
    out_ref[rows:, :] = second_ref[...]


def sum_kernel(count, *refs):
    parts, outs = refs[:count], refs[count:]
    rows, width = outs[0].shape
    across = parts[0].shape[1] // width
    for i, out in enumerate(outs):
        here = (slice((i // across) * rows, (i // across + 1) * rows), slice((i % across) * width, (i % across + 1) * width))
        value = parts[0][here]
        for part in parts[1:]:
            value = value + part[here]
        out[...] = value


def choose_kernel(segment_ref, own_ref, shifted_ref, out_ref, held, arrived, left):
    steps = arrived.shape[0]
    rows = own_ref.shape[0] // steps
    parts = [slice(q * rows, (q + 1) * rows) for q in range(steps)]
    outs = [pltpu.make_async_copy(held.at[p], out_ref.at[p], left.at[q]) for q, p in enumerate(parts)]

    def through(source):
        ins = [pltpu.make_async_copy(source.at[p], held.at[p], arrived.at[q]) for q, p in enumerate(parts)]
        for copy in ins:
            copy.start()
        for come, go in zip(ins, outs):
            come.wait()
            go.start()

    pl.when(segment_ref[0] == 0)(lambda: through(own_ref))
    pl.when(segment_ref[0] != 0)(lambda: through(shifted_ref))
    for copy in outs:
        copy.wait()


def passed_along(value, axis, steps):
    count = lax.axis_size(axis)
    first, last = (max(0, -steps), min(count, count - steps))
    return lax.ppermute(value, axis, [(source, source + steps) for source in range(first, last)])


def near(value):
    return pltpu.with_memory_space_constraint(value, pltpu.VMEM)


def far(value):
    return pltpu.with_memory_space_constraint(value, pltpu.HBM)


def swapped(value, axis, mask):
    count = lax.axis_size(axis)
    return near(lax.ppermute(value, axis, [(source, source ^ mask) for source in range(count)]))


def call(kernel, ins, outs, scratch, *operands, params=SMALL):
    return pl.pallas_call(
        kernel,
        in_specs=ins,
        out_specs=[VMEM] * len(outs),
        out_shape=outs,
        scratch_shapes=scratch,
        compiler_params=params,
    )(*operands)


def summed(shape, *parts):
    size = parts[0].shape
    outs = [pltpu.VMEM(shape, F32)] * ((size[0] // shape[0]) * (size[1] // shape[1]))
    return call(functools.partial(sum_kernel, len(parts)), [VMEM] * len(parts), outs, [], *parts)


def all_steps(
    left_ops,
    right_ops,
    wavefunction,
    basis_rotation,
    pair_term,
    coupling,
    left_charge,
    right_charge,
):
    own_left = left_ops[0, 0]
    own_right = right_ops[0, 0]
    rows, size = wavefunction.shape[1:]
    block = size // NQ
    count = lax.axis_size("op")
    group = count // 2
    me = jnp.reshape(lax.axis_index("op").astype(jnp.int32), (1,))

    (packed,) = call(
        pack_kernel,
        [SMEM, HBM, HBM, HBM],
        [pltpu.VMEM((rows, block), F32)],
        [
            pltpu.VMEM((size, LANES), F32),
            pltpu.VMEM((1, size), jnp.int32),
            pltpu.VMEM((1, size), jnp.int32),
            pltpu.VMEM((rows, size), F32),
            pltpu.SemaphoreType.DMA((3,)),
        ],
        me,
        far(left_charge),
        far(right_charge),
        far(wavefunction[0]),
    )
    (pair,) = call(
        join_kernel, [VMEM] * 2, [pltpu.VMEM((2 * rows, block), F32)], [], packed, swapped(packed, "op", group)
    )
    gathered = [pair] + [swapped(pair, "op", s) for s in range(1, group)]

    left_half_high, left_half_low, onto, back, left_column = sort_columns(left_charge, own_left)
    left_high, left_low, right_high, right_low = sort_rest(right_charge, left_half_high, left_half_low, onto, own_right)
    pieces = (left_high, left_low, right_high, right_low)
    halves = [pltpu.VMEM((size, size), BF16), pltpu.VMEM((size, size), BF16), pltpu.VMEM((size, block), F32)]
    pairs = [pltpu.VMEM((2 * rows, block), F32)] * group

    initial, initial_rows, *sent = call(
        functools.partial(first_kernel, group),
        [SMEM, SMEM, SMEM] + [VMEM] * (group + 5),
        [pltpu.VMEM((size, block), F32), pltpu.VMEM((rows, block), F32)] + pairs,
        halves,
        me,
        pair_term,
        coupling,
        onto,
        *gathered,
        *pieces,
        params=LIMIT,
    )
    inner = range(group - 1, 0, -1)
    wings = [pltpu.VMEM((2 * rows, block // 2), F32)] * (2 * group)
    totals = summed((2 * rows, block // 2), sent[0], *[swapped(sent[s], "op", s) for s in inner])
    across = [swapped(total, "op", group) for total in totals]
    gathered = []
    for c in range(2):
        (total,) = summed((2 * rows, block // 2), totals[c], across[c])
        gathered += [total] + [swapped(total, "op", s) for s in inner][::-1]

    energy, spread, step_rows, spot, *sent = call(
        functools.partial(second_kernel, group),
        [SMEM, SMEM, SMEM] + [VMEM] * (2 * group + 7),
        [
            pltpu.VMEM((1, 1), F32),
            pltpu.VMEM((1, 1), F32),
            pltpu.VMEM((rows, block), F32),
            pltpu.VMEM((rows, LANES), F32),
        ]
        + wings,
        halves + [pltpu.VMEM((size, block), F32)],
        me,
        pair_term,
        coupling,
        back,
        near(left_column),
        *gathered,
        initial,
        *pieces,
        params=LIMIT,
    )
    kept, received = [], []
    for c in range(2):
        mine = sent[c * group : (c + 1) * group]
        keep, away = summed((rows, block // 2), near(mine[0]), *[swapped(mine[s], "op", s) for s in inner])
        kept.append(near(keep))
        received.append(swapped(away, "op", group))
    (right_onto,) = call(
        order_kernel, [VMEM], [pltpu.VMEM((size, size), BF16)], [], far(right_charge)
    )
    (chebyshev,) = call(
        last_kernel,
        [VMEM] * 10,
        [jax.ShapeDtypeStruct((rows, size), F32)],
        [],
        near(spot),
        near(right_onto),
        near(energy),
        near(spread),
        near(initial_rows),
        near(step_rows),
        *kept,
        *received,
    )

    turned_left, _ = lax.optimization_barrier((own_left, initial))
    half_turn = jnp.dot(turned_left, basis_rotation[0], precision=lax.Precision.HIGH)
    rotated = lax.dot_general(
        basis_rotation[0], half_turn, (((0,), (0,)), ((), ())), precision=lax.Precision.HIGH
    )
    shifted = passed_along(far(rotated), "seg", 1)
    segment = jnp.reshape(lax.axis_index("seg").astype(jnp.int32), (1,))
    handed = pl.pallas_call(
        choose_kernel,
        in_specs=[SMEM, HBM, HBM],
        out_specs=HBM,
        out_shape=jax.ShapeDtypeStruct((size, size), F32),
        scratch_shapes=[
            pltpu.VMEM((size, size), F32),
            pltpu.SemaphoreType.DMA((4 * NQ,)),
            pltpu.SemaphoreType.DMA((4 * NQ,)),
        ],
        compiler_params=SMALL,
    )(segment, far(own_left), far(shifted))[None, None]
    return (chebyshev[None], energy[0], handed)


def solution(mesh):
    placed = (
        P("seg", "op", None, None),
        P("seg", "op", None, None),
        P("seg", "op", None),
        P("seg", None, None),
        P("seg", "op"),
        P(),
        P("seg", None),
        P("seg", None),
    )
    return jax.shard_map(
        all_steps,
        mesh=mesh,
        in_specs=placed,
        out_specs=(P("seg", "op", None), P("seg"), P("seg", "op", None, None)),
        check_vma=False,
    )
```

```python
import functools

import jax
import jax.numpy as jnp
from jax import lax
from jax.experimental import pallas as pl
from jax.experimental.pallas import tpu as pltpu
from jax.sharding import PartitionSpec as P


NQ = 3
F32 = jnp.float32
BF16 = jnp.bfloat16
LANES = 128


VMEM = pl.BlockSpec(memory_space=pltpu.VMEM)
SMEM = pl.BlockSpec(memory_space=pltpu.SMEM)
HBM = pl.BlockSpec(memory_space=pltpu.HBM)
LIMIT = pltpu.CompilerParams(vmem_limit_bytes=16 << 20)
SMALL = pltpu.CompilerParams(vmem_limit_bytes=4 << 20)


def mm(a, b):
    return lax.dot_general(a, b, (((1,), (0,)), ((), ())), preferred_element_type=F32)


def split(x):
    high = x.astype(BF16)
    return high, (x - high.astype(F32)).astype(BF16)


def mm3(ah, al, bh, bl):
    return mm(ah, bh) + (mm(ah, bl) + mm(al, bh))


def places_of(charge, block):
    size = charge.shape[1]
    own = (lax.broadcasted_iota(jnp.int32, (16, size), 0) == charge).astype(F32)
    earlier = lax.broadcasted_iota(jnp.int32, (LANES, LANES), 0) < lax.broadcasted_iota(jnp.int32, (LANES, LANES), 1)
    earlier = earlier.astype(F32).astype(BF16)
    before = jnp.zeros((16, 1), F32)
    ranks = []
    for c in range(size // LANES):
        part = own[:, c * LANES : (c + 1) * LANES]
        counts = mm(part.astype(BF16), earlier) + before
        ranks.append(jnp.sum(part * counts, axis=0, keepdims=True))
        before = before + jnp.sum(part, axis=1, keepdims=True)
    return jnp.concatenate(ranks, axis=1) + (charge * block).astype(F32)


def chosen(places, positions):
    return jnp.where(places.astype(BF16) == positions, jnp.ones((), BF16), jnp.zeros((), BF16))


def sorter(place_row):
    size = place_row.shape[1]
    step = 2 * LANES
    place = lax.broadcasted_iota(jnp.int32, (step, size), 0).astype(F32).astype(BF16)
    row = jnp.broadcast_to(place_row, (step, size))
    return jnp.concatenate([chosen(row - float(c), place) for c in range(0, size, step)], axis=0)


def column(row):
    return jnp.transpose(jnp.broadcast_to(row, (LANES, row.shape[1])))


def unsorter(place_column, size):
    lane = lax.broadcasted_iota(jnp.int32, place_column.shape, 1).astype(F32).astype(BF16)
    return jnp.concatenate([chosen(place_column - float(c), lane) for c in range(0, size, LANES)], axis=1)


def pack_kernel(
    me_ref, left_hbm, right_hbm, wave_hbm, packed_ref, column_ref, left_ref, right_ref, wave_ref, arrived
):
    rows, size = wave_ref.shape
    block = size // NQ
    copies = [
        pltpu.make_async_copy(source, target, arrived.at[i])
        for i, (source, target) in enumerate(
            ((right_hbm, right_ref), (left_hbm, left_ref), (wave_hbm, wave_ref))
        )
    ]
    for copy in copies:
        copy.start()
    copies[0].wait()
    back = unsorter(column(places_of(right_ref[...], block)), size)
    copies[1].wait()
    column_ref[...] = column(left_ref[...].astype(F32))
    start = pl.multiple_of(me_ref[0] * rows, 8)
    charge = column_ref[pl.ds(start, rows), :][:, :1]
    copies[2].wait()
    both = mm(jnp.concatenate(split(wave_ref[...]), axis=0), back)
    ordered = both[:rows, :] + both[rows:, :]
    packed = jnp.zeros((rows, block), F32)
    for q in range(NQ):
        packed = packed + jnp.where(charge == float(q), ordered[:, q * block : (q + 1) * block], 0.0)
    packed_ref[...] = packed


def columns_kernel(charge_ref, ops_ref, half_high, half_low, onto, back, column_ref):
    rows, size = ops_ref.shape
    step = pl.program_id(0)

    @pl.when(step == 0)
    def _():
        place = places_of(charge_ref[...], size // NQ)
        column_ref[...] = column(place)
        onto[...] = sorter(place)
        back[...] = unsorter(column_ref[...], size)

    high, low = split(ops_ref[...])
    here = pl.ds(pl.multiple_of(step * rows, rows), rows)
    half_high[here, :] = mm(high, back[...]).astype(BF16)
    half_low[here, :] = mm(low, back[...]).astype(BF16)


def sort_kernel(
    charge_ref,
    left_half_high,
    left_half_low,
    left_onto,
    ops_ref,
    left_high,
    left_low,
    right_high,
    right_low,
    onto,
    back,
    half_high,
    half_low,
):
    rows, size = ops_ref.shape
    step = pl.program_id(0)

    @pl.when(step == 0)
    def _():
        place = places_of(charge_ref[...], size // NQ)
        onto[...] = sorter(place)
        back[...] = unsorter(column(place), size)

    here = pl.ds(pl.multiple_of(step * rows, rows), rows)
    left_high[here, :] = mm(left_onto[here, :], left_half_high[...]).astype(BF16)
    left_low[here, :] = mm(left_onto[here, :], left_half_low[...]).astype(BF16)
    high, low = split(ops_ref[...])
    half_high[here, :] = mm(high, back[...]).astype(BF16)
    half_low[here, :] = mm(low, back[...]).astype(BF16)

    @pl.when(step == pl.num_programs(0) - 1)
    def _():
        for q in range(NQ):
            there = slice(q * rows, (q + 1) * rows)
            right_high[there, :] = mm(onto[there, :], half_high[...]).astype(BF16)
            right_low[there, :] = mm(onto[there, :], half_low[...]).astype(BF16)


def sort_columns(charge, ops):
    size = ops.shape[0]
    rows = size // NQ
    return pl.pallas_call(
        columns_kernel,
        grid=(NQ,),
        in_specs=[VMEM, pl.BlockSpec((rows, size), lambda i: (i, 0))],
        out_specs=[VMEM] * 5,
        out_shape=[pltpu.VMEM((size, size), BF16)] * 4 + [pltpu.VMEM((size, LANES), F32)],
        compiler_params=LIMIT,
    )(far(charge), far(ops))


def sort_rest(charge, left_half_high, left_half_low, left_onto, ops):
    size = ops.shape[0]
    rows = size // NQ
    return pl.pallas_call(
        sort_kernel,
        grid=(NQ,),
        in_specs=[VMEM] * 4 + [pl.BlockSpec((rows, size), lambda i: (i, 0))],
        out_specs=[VMEM] * 4,
        out_shape=[pltpu.VMEM((size, size), BF16)] * 4,
        scratch_shapes=[pltpu.VMEM((size, size), BF16) for _ in range(4)],
        compiler_params=LIMIT,
    )(far(charge), left_half_high, left_half_low, left_onto, far(ops))


def apply_blocks(packed, scale, left_high, left_low, right_high, right_low, half_high, half_low, total):
    block = packed.shape[1]
    for q in range(NQ):
        here = slice(q * block, (q + 1) * block)
        high, low = split(packed[here, :])
        value = mm3(left_high[:, here], left_low[:, here], high, low) * scale
        half_high[:, here], half_low[:, here] = split(value)
    for q in range(NQ):
        here = slice(q * block, (q + 1) * block)
        total[here, :] = mm3(half_high[here, :], half_low[here, :], right_high[:, here], right_low[:, here])


def first_kernel(group, me_ref, term_ref, table_ref, onto_ref, *refs):
    parts = refs[:group]
    left_high, left_low, right_high, right_low = refs[group : group + 4]
    initial_ref, initial_rows_ref = refs[group + 4 : group + 6]
    outs = refs[group + 6 : 2 * group + 6]
    half_high, half_low, total = refs[2 * group + 6 :]
    half = lax.div(me_ref[0], group)
    own = lax.rem(me_ref[0], group)
    pair, block = parts[0].shape
    rows = pair // 2
    size = pair * group
    for s in range(group):
        for h, side in enumerate((half, 1 - half)):
            start = pl.multiple_of((side * group + (own ^ s)) * rows, 8)
            total[pl.ds(start, rows), :] = parts[s][h * rows : (h + 1) * rows, :]
    high, low = split(total[...])
    packed = mm(onto_ref[...], high) + mm(onto_ref[...], low)
    norm = jnp.sqrt(jnp.sum(packed * packed, keepdims=True) / float(size * size) + 1e-06)
    initial_ref[...] = packed / norm
    initial_rows_ref[...] = parts[0][:rows, :] / norm
    scale = table_ref[term_ref[0, 0]]
    apply_blocks(
        initial_ref[...], scale, left_high, left_low, right_high, right_low, half_high, half_low, total
    )
    each = block // group
    for s in range(group):
        for q in range(NQ):
            start = pl.multiple_of(q * block + (own ^ s) * each, 8)
            outs[s][q * each : (q + 1) * each, :] = total[pl.ds(start, each), :]


def second_kernel(group, me_ref, term_ref, table_ref, back_ref, column_ref, *refs):
    count = 2 * group
    parts = refs[:count]
    initial_ref, left_high, left_low, right_high, right_low = refs[count : count + 5]
    energy_ref, spread_ref, step_rows_ref, spot_ref = refs[count + 5 : count + 9]
    outs = refs[count + 9 : 2 * count + 9]
    half_high, half_low, total, step_ref = refs[2 * count + 9 :]
    half = lax.div(me_ref[0], group)
    own = lax.rem(me_ref[0], group)
    pair, width = parts[0].shape
    block = 2 * width
    sides = [slice(c * width, (c + 1) * width) for c in range(2)]
    rows = pair // 2
    size = pair * group
    each = block // group
    for s in range(group):
        for q in range(NQ):
            start = pl.multiple_of(q * block + (own ^ s) * each, 8)
            for c in range(2):
                total[pl.ds(start, each), sides[c]] = parts[c * group + s][q * each : (q + 1) * each, :]
    cells = float(size * size)
    energy = jnp.sum(initial_ref[...] * total[...], keepdims=True) / cells
    spread = jnp.sqrt(jnp.sum(total[...] * total[...], keepdims=True) / cells + 1e-06)
    step_ref[...] = (total[...] - energy * initial_ref[...]) / spread
    energy_ref[...] = energy
    spread_ref[...] = spread
    scale = table_ref[term_ref[0, 0]]
    apply_blocks(
        step_ref[...], scale, left_high, left_low, right_high, right_low, half_high, half_low, total
    )
    high, low = split(total[...])
    total[...] = mm(back_ref[...], high) + mm(back_ref[...], low)
    start = pl.multiple_of(me_ref[0] * rows, 8)
    spot_ref[...] = column_ref[pl.ds(start, rows), :]
    back = unsorter(spot_ref[...], size)
    high, low = split(step_ref[...])
    step_rows_ref[...] = mm(back, high) + mm(back, low)
    for s in range(group):
        for h, side in enumerate((half, 1 - half)):
            start = pl.multiple_of((side * group + (own ^ s)) * rows, 8)
            for c in range(2):
                outs[c * group + s][h * rows : (h + 1) * rows, :] = total[pl.ds(start, rows), sides[c]]


def order_kernel(charge_ref, onto_ref):
    onto_ref[...] = sorter(places_of(charge_ref[...], charge_ref.shape[1] // NQ))


def last_kernel(spot_ref, onto_ref, energy_ref, spread_ref, initial_ref, step_ref, *refs):
    kept, sent, out_ref = refs[:2], refs[2:4], refs[4]
    image = jnp.concatenate([a[...] + b[...] for a, b in zip(kept, sent)], axis=1)
    packed = 2.0 * (image - energy_ref[...] * step_ref[...]) / spread_ref[...] - initial_ref[...]
    block = packed.shape[1]
    spot = jnp.broadcast_to(spot_ref[...][:, :1], packed.shape)
    held = [(spot >= float(q * block)) & (spot < float((q + 1) * block)) for q in range(NQ)]
    high = packed.astype(BF16).astype(F32)
    wide = [
        jnp.concatenate([jnp.where(here, piece, 0.0) for here in held], axis=1) for piece in (high, packed - high)
    ]
    both = mm(jnp.concatenate(wide, axis=0).astype(BF16), onto_ref[...])
    rows = packed.shape[0]
    out_ref[...] = both[:rows, :] + both[rows:, :]


def join_kernel(first_ref, second_ref, out_ref):
    rows = first_ref.shape[0]
    out_ref[:rows, :] = first_ref[...]
    out_ref[rows:, :] = second_ref[...]


def sum_kernel(count, *refs):
    parts, outs = refs[:count], refs[count:]
    rows, width = outs[0].shape
    across = parts[0].shape[1] // width
    for i, out in enumerate(outs):
        here = (slice((i // across) * rows, (i // across + 1) * rows), slice((i % across) * width, (i % across + 1) * width))
        value = parts[0][here]
        for part in parts[1:]:
            value = value + part[here]
        out[...] = value


def choose_kernel(segment_ref, own_ref, shifted_ref, out_ref, held, arrived, left):
    steps = arrived.shape[0]
    rows = own_ref.shape[0] // steps
    parts = [slice(q * rows, (q + 1) * rows) for q in range(steps)]

    @pl.when(segment_ref[0] == 0)
    def _():
        ins = [pltpu.make_async_copy(own_ref.at[p], held.at[p], arrived.at[q]) for q, p in enumerate(parts)]
        outs = [pltpu.make_async_copy(held.at[p], out_ref.at[p], left.at[q]) for q, p in enumerate(parts)]
        for copy in ins:
            copy.start()
        for come, go in zip(ins, outs):
            come.wait()
            go.start()
        for copy in outs:
            copy.wait()

    @pl.when(segment_ref[0] != 0)
    def _():
        copy = pltpu.make_async_copy(shifted_ref, out_ref, left.at[0])
        copy.start()
        copy.wait()


def passed_along(value, axis, steps):
    count = lax.axis_size(axis)
    first, last = (max(0, -steps), min(count, count - steps))
    return lax.ppermute(value, axis, [(source, source + steps) for source in range(first, last)])


def near(value):
    return pltpu.with_memory_space_constraint(value, pltpu.VMEM)


def far(value):
    return pltpu.with_memory_space_constraint(value, pltpu.HBM)


def swapped(value, axis, mask):
    count = lax.axis_size(axis)
    return near(lax.ppermute(value, axis, [(source, source ^ mask) for source in range(count)]))


def call(kernel, ins, outs, scratch, *operands, params=SMALL):
    return pl.pallas_call(
        kernel,
        in_specs=ins,
        out_specs=[VMEM] * len(outs),
        out_shape=outs,
        scratch_shapes=scratch,
        compiler_params=params,
    )(*operands)


def summed(shape, *parts):
    size = parts[0].shape
    outs = [pltpu.VMEM(shape, F32)] * ((size[0] // shape[0]) * (size[1] // shape[1]))
    return call(functools.partial(sum_kernel, len(parts)), [VMEM] * len(parts), outs, [], *parts)


def all_steps(
    left_ops,
    right_ops,
    wavefunction,
    basis_rotation,
    pair_term,
    coupling,
    left_charge,
    right_charge,
):
    own_left = left_ops[0, 0]
    own_right = right_ops[0, 0]
    rows, size = wavefunction.shape[1:]
    block = size // NQ
    count = lax.axis_size("op")
    group = count // 2
    me = jnp.reshape(lax.axis_index("op").astype(jnp.int32), (1,))
    segment = jnp.reshape(lax.axis_index("seg").astype(jnp.int32), (1,))
    me, segment = lax.optimization_barrier((me, segment))

    (packed,) = call(
        pack_kernel,
        [SMEM, HBM, HBM, HBM],
        [pltpu.VMEM((rows, block), F32)],
        [
            pltpu.VMEM((size, LANES), F32),
            pltpu.VMEM((1, size), jnp.int32),
            pltpu.VMEM((1, size), jnp.int32),
            pltpu.VMEM((rows, size), F32),
            pltpu.SemaphoreType.DMA((3,)),
        ],
        me,
        far(left_charge),
        far(right_charge),
        far(wavefunction[0]),
    )
    (pair,) = call(
        join_kernel, [VMEM] * 2, [pltpu.VMEM((2 * rows, block), F32)], [], packed, swapped(packed, "op", group)
    )
    gathered = [pair] + [swapped(pair, "op", s) for s in range(1, group)]

    left_half_high, left_half_low, onto, back, left_column = sort_columns(left_charge, own_left)
    left_high, left_low, right_high, right_low = sort_rest(right_charge, left_half_high, left_half_low, onto, own_right)
    pieces = (left_high, left_low, right_high, right_low)
    halves = [pltpu.VMEM((size, size), BF16), pltpu.VMEM((size, size), BF16), pltpu.VMEM((size, block), F32)]
    pairs = [pltpu.VMEM((2 * rows, block), F32)] * group

    initial, initial_rows, *sent = call(
        functools.partial(first_kernel, group),
        [SMEM, SMEM, SMEM] + [VMEM] * (group + 5),
        [pltpu.VMEM((size, block), F32), pltpu.VMEM((rows, block), F32)] + pairs,
        halves,
        me,
        pair_term,
        coupling,
        onto,
        *gathered,
        *pieces,
        params=LIMIT,
    )
    inner = range(group - 1, 0, -1)
    wings = [pltpu.VMEM((2 * rows, block // 2), F32)] * (2 * group)
    totals = summed((2 * rows, block // 2), sent[0], *[swapped(sent[s], "op", s) for s in inner])
    across = [swapped(total, "op", group) for total in totals]
    gathered = []
    for c in range(2):
        (total,) = summed((2 * rows, block // 2), totals[c], across[c])
        gathered += [total] + [swapped(total, "op", s) for s in inner][::-1]

    energy, spread, step_rows, spot, *sent = call(
        functools.partial(second_kernel, group),
        [SMEM, SMEM, SMEM] + [VMEM] * (2 * group + 7),
        [
            pltpu.VMEM((1, 1), F32),
            pltpu.VMEM((1, 1), F32),
            pltpu.VMEM((rows, block), F32),
            pltpu.VMEM((rows, LANES), F32),
        ]
        + wings,
        halves + [pltpu.VMEM((size, block), F32)],
        me,
        pair_term,
        coupling,
        back,
        near(left_column),
        *gathered,
        initial,
        *pieces,
        params=LIMIT,
    )
    kept, received = [], []
    for c in range(2):
        mine = sent[c * group : (c + 1) * group]
        keep, away = summed((rows, block // 2), near(mine[0]), *[swapped(mine[s], "op", s) for s in inner])
        kept.append(near(keep))
        received.append(swapped(away, "op", group))
    (right_onto,) = call(
        order_kernel, [VMEM], [pltpu.VMEM((size, size), BF16)], [], far(right_charge)
    )
    (chebyshev,) = call(
        last_kernel,
        [VMEM] * 10,
        [jax.ShapeDtypeStruct((rows, size), F32)],
        [],
        near(spot),
        near(right_onto),
        near(energy),
        near(spread),
        near(initial_rows),
        near(step_rows),
        *kept,
        *received,
    )

    turned_left, _ = lax.optimization_barrier((own_left, initial))
    half_turn = jnp.dot(turned_left, basis_rotation[0], precision=lax.Precision.HIGH)
    rotated = lax.dot_general(
        basis_rotation[0], half_turn, (((0,), (0,)), ((), ())), precision=lax.Precision.HIGH
    )
    shifted = passed_along(far(rotated), "seg", 1)
    handed = pl.pallas_call(
        choose_kernel,
        in_specs=[SMEM, HBM, VMEM],
        out_specs=HBM,
        out_shape=jax.ShapeDtypeStruct((size, size), F32),
        scratch_shapes=[
            pltpu.VMEM((size, size), F32),
            pltpu.SemaphoreType.DMA((4 * NQ,)),
            pltpu.SemaphoreType.DMA((4 * NQ,)),
        ],
        compiler_params=SMALL,
    )(segment, far(own_left), near(shifted))[None, None]
    return (chebyshev[None], energy[0], handed)


def solution(mesh):
    placed = (
        P("seg", "op", None, None),
        P("seg", "op", None, None),
        P("seg", "op", None),
        P("seg", None, None),
        P("seg", "op"),
        P(),
        P("seg", None),
        P("seg", None),
    )
    return jax.shard_map(
        all_steps,
        mesh=mesh,
        in_specs=placed,
        out_specs=(P("seg", "op", None), P("seg"), P("seg", "op", None, None)),
        check_vma=False,
    )
```

```python
import functools

import jax
import jax.numpy as jnp
from jax import lax
from jax.experimental import pallas as pl
from jax.experimental.pallas import tpu as pltpu
from jax.sharding import PartitionSpec as P


NQ = 3
F32 = jnp.float32
BF16 = jnp.bfloat16
LANES = 128


VMEM = pl.BlockSpec(memory_space=pltpu.VMEM)
SMEM = pl.BlockSpec(memory_space=pltpu.SMEM)
HBM = pl.BlockSpec(memory_space=pltpu.HBM)
LIMIT = pltpu.CompilerParams(vmem_limit_bytes=16 << 20)
SMALL = pltpu.CompilerParams(vmem_limit_bytes=4 << 20)


def mm(a, b):
    return lax.dot_general(a, b, (((1,), (0,)), ((), ())), preferred_element_type=F32)


def split(x):
    high = x.astype(BF16)
    return high, (x - high.astype(F32)).astype(BF16)


def mm3(ah, al, bh, bl):
    return mm(ah, bh) + (mm(ah, bl) + mm(al, bh))


def places_of(charge, block):
    size = charge.shape[1]
    own = (lax.broadcasted_iota(jnp.int32, (16, size), 0) == charge).astype(F32)
    earlier = lax.broadcasted_iota(jnp.int32, (LANES, LANES), 0) < lax.broadcasted_iota(jnp.int32, (LANES, LANES), 1)
    earlier = earlier.astype(F32).astype(BF16)
    before = jnp.zeros((16, 1), F32)
    ranks = []
    for c in range(size // LANES):
        part = own[:, c * LANES : (c + 1) * LANES]
        counts = mm(part.astype(BF16), earlier) + before
        ranks.append(jnp.sum(part * counts, axis=0, keepdims=True))
        before = before + jnp.sum(part, axis=1, keepdims=True)
    return jnp.concatenate(ranks, axis=1) + (charge * block).astype(F32)


def chosen(places, positions):
    return jnp.where(places.astype(BF16) == positions, jnp.ones((), BF16), jnp.zeros((), BF16))


def sorter(place_row):
    size = place_row.shape[1]
    step = 2 * LANES
    place = lax.broadcasted_iota(jnp.int32, (step, size), 0).astype(F32).astype(BF16)
    row = jnp.broadcast_to(place_row, (step, size))
    return jnp.concatenate([chosen(row - float(c), place) for c in range(0, size, step)], axis=0)


def column(row):
    return jnp.transpose(jnp.broadcast_to(row, (LANES, row.shape[1])))


def unsorter(place_column, size):
    lane = lax.broadcasted_iota(jnp.int32, place_column.shape, 1).astype(F32).astype(BF16)
    return jnp.concatenate([chosen(place_column - float(c), lane) for c in range(0, size, LANES)], axis=1)


def pack_kernel(
    me_ref, left_hbm, right_hbm, wave_hbm, packed_ref, column_ref, left_ref, right_ref, wave_ref, arrived
):
    rows, size = wave_ref.shape
    block = size // NQ
    copies = [
        pltpu.make_async_copy(source, target, arrived.at[i])
        for i, (source, target) in enumerate(
            ((right_hbm, right_ref), (left_hbm, left_ref), (wave_hbm, wave_ref))
        )
    ]
    for copy in copies:
        copy.start()
    copies[0].wait()
    back = unsorter(column(places_of(right_ref[...], block)), size)
    copies[1].wait()
    column_ref[...] = column(left_ref[...].astype(F32))
    start = pl.multiple_of(me_ref[0] * rows, 8)
    charge = column_ref[pl.ds(start, rows), :][:, :1]
    copies[2].wait()
    both = mm(jnp.concatenate(split(wave_ref[...]), axis=0), back)
    ordered = both[:rows, :] + both[rows:, :]
    packed = jnp.zeros((rows, block), F32)
    for q in range(NQ):
        packed = packed + jnp.where(charge == float(q), ordered[:, q * block : (q + 1) * block], 0.0)
    packed_ref[...] = packed


def columns_kernel(charge_ref, ops_ref, half_high, half_low, onto, back, column_ref):
    rows, size = ops_ref.shape
    step = pl.program_id(0)

    @pl.when(step == 0)
    def _():
        place = places_of(charge_ref[...], size // NQ)
        column_ref[...] = column(place)
        onto[...] = sorter(place)
        back[...] = unsorter(column_ref[...], size)

    high, low = split(ops_ref[...])
    here = pl.ds(pl.multiple_of(step * rows, rows), rows)
    half_high[here, :] = mm(high, back[...]).astype(BF16)
    half_low[here, :] = mm(low, back[...]).astype(BF16)


def sort_kernel(
    charge_ref,
    left_half_high,
    left_half_low,
    left_onto,
    ops_ref,
    left_high,
    left_low,
    right_high,
    right_low,
    onto,
    back,
    half_high,
    half_low,
):
    rows, size = ops_ref.shape
    step = pl.program_id(0)

    @pl.when(step == 0)
    def _():
        place = places_of(charge_ref[...], size // NQ)
        onto[...] = sorter(place)
        back[...] = unsorter(column(place), size)

    here = pl.ds(pl.multiple_of(step * rows, rows), rows)
    left_high[here, :] = mm(left_onto[here, :], left_half_high[...]).astype(BF16)
    left_low[here, :] = mm(left_onto[here, :], left_half_low[...]).astype(BF16)
    high, low = split(ops_ref[...])
    half_high[here, :] = mm(high, back[...]).astype(BF16)
    half_low[here, :] = mm(low, back[...]).astype(BF16)

    @pl.when(step == pl.num_programs(0) - 1)
    def _():
        for q in range(NQ):
            there = slice(q * rows, (q + 1) * rows)
            right_high[there, :] = mm(onto[there, :], half_high[...]).astype(BF16)
            right_low[there, :] = mm(onto[there, :], half_low[...]).astype(BF16)


def sort_columns(charge, ops):
    size = ops.shape[0]
    rows = size // NQ
    return pl.pallas_call(
        columns_kernel,
        grid=(NQ,),
        in_specs=[VMEM, pl.BlockSpec((rows, size), lambda i: (i, 0))],
        out_specs=[VMEM] * 5,
        out_shape=[pltpu.VMEM((size, size), BF16)] * 4 + [pltpu.VMEM((size, LANES), F32)],
        compiler_params=LIMIT,
    )(far(charge), far(ops))


def sort_rest(charge, left_half_high, left_half_low, left_onto, ops):
    size = ops.shape[0]
    rows = size // NQ
    return pl.pallas_call(
        sort_kernel,
        grid=(NQ,),
        in_specs=[VMEM] * 4 + [pl.BlockSpec((rows, size), lambda i: (i, 0))],
        out_specs=[VMEM] * 4,
        out_shape=[pltpu.VMEM((size, size), BF16)] * 4,
        scratch_shapes=[pltpu.VMEM((size, size), BF16) for _ in range(4)],
        compiler_params=LIMIT,
    )(far(charge), left_half_high, left_half_low, left_onto, far(ops))


def apply_blocks(packed, scale, left_high, left_low, right_high, right_low, halfs, total):
    block = packed.shape[1]
    for q in range(NQ):
        here = slice(q * block, (q + 1) * block)
        high, low = split(packed[here, :])
        value = mm3(left_high[:, here], left_low[:, here], high, low) * scale
        high, low = split(value)
        for o in range(NQ):
            there = slice(o * block, (o + 1) * block)
            halfs[2 * o * block : (2 * o + 1) * block, here] = high[there, :]
            halfs[(2 * o + 1) * block : 2 * (o + 1) * block, here] = low[there, :]
    for q in range(NQ):
        here = slice(q * block, (q + 1) * block)
        both = mm(halfs[2 * q * block : 2 * (q + 1) * block, :], right_high[:, here])
        rest = mm(halfs[2 * q * block : (2 * q + 1) * block, :], right_low[:, here])
        total[here, :] = both[:block, :] + (both[block:, :] + rest)


def first_kernel(group, me_ref, term_ref, table_ref, onto_ref, *refs):
    parts = refs[:group]
    left_high, left_low, right_high, right_low = refs[group : group + 4]
    initial_ref, initial_rows_ref = refs[group + 4 : group + 6]
    outs = refs[group + 6 : 2 * group + 6]
    halfs, total = refs[2 * group + 6 :]
    half = lax.div(me_ref[0], group)
    own = lax.rem(me_ref[0], group)
    pair, block = parts[0].shape
    rows = pair // 2
    size = pair * group
    for s in range(group):
        for h, side in enumerate((half, 1 - half)):
            start = pl.multiple_of((side * group + (own ^ s)) * rows, 8)
            total[pl.ds(start, rows), :] = parts[s][h * rows : (h + 1) * rows, :]
    high, low = split(total[...])
    packed = mm(onto_ref[...], high) + mm(onto_ref[...], low)
    norm = jnp.sqrt(jnp.sum(packed * packed, keepdims=True) / float(size * size) + 1e-06)
    initial_ref[...] = packed / norm
    initial_rows_ref[...] = parts[0][:rows, :] / norm
    scale = table_ref[term_ref[0, 0]]
    apply_blocks(
        initial_ref[...], scale, left_high, left_low, right_high, right_low, halfs, total
    )
    each = block // group
    for s in range(group):
        for q in range(NQ):
            start = pl.multiple_of(q * block + (own ^ s) * each, 8)
            outs[s][q * each : (q + 1) * each, :] = total[pl.ds(start, each), :]


def second_kernel(group, me_ref, term_ref, table_ref, back_ref, column_ref, *refs):
    count = 2 * group
    parts = refs[:count]
    initial_ref, left_high, left_low, right_high, right_low = refs[count : count + 5]
    energy_ref, spread_ref, step_rows_ref, spot_ref = refs[count + 5 : count + 9]
    outs = refs[count + 9 : 2 * count + 9]
    halfs, total, step_ref = refs[2 * count + 9 :]
    half = lax.div(me_ref[0], group)
    own = lax.rem(me_ref[0], group)
    pair, width = parts[0].shape
    block = 2 * width
    sides = [slice(c * width, (c + 1) * width) for c in range(2)]
    rows = pair // 2
    size = pair * group
    each = block // group
    for s in range(group):
        for q in range(NQ):
            start = pl.multiple_of(q * block + (own ^ s) * each, 8)
            for c in range(2):
                total[pl.ds(start, each), sides[c]] = parts[c * group + s][q * each : (q + 1) * each, :]
    cells = float(size * size)
    energy = jnp.sum(initial_ref[...] * total[...], keepdims=True) / cells
    spread = jnp.sqrt(jnp.sum(total[...] * total[...], keepdims=True) / cells + 1e-06)
    step_ref[...] = (total[...] - energy * initial_ref[...]) / spread
    energy_ref[...] = energy
    spread_ref[...] = spread
    scale = table_ref[term_ref[0, 0]]
    apply_blocks(
        step_ref[...], scale, left_high, left_low, right_high, right_low, halfs, total
    )
    high, low = split(total[...])
    total[...] = mm(back_ref[...], high) + mm(back_ref[...], low)
    start = pl.multiple_of(me_ref[0] * rows, 8)
    spot_ref[...] = column_ref[pl.ds(start, rows), :]
    back = unsorter(spot_ref[...], size)
    high, low = split(step_ref[...])
    step_rows_ref[...] = mm(back, high) + mm(back, low)
    for s in range(group):
        for h, side in enumerate((half, 1 - half)):
            start = pl.multiple_of((side * group + (own ^ s)) * rows, 8)
            for c in range(2):
                outs[c * group + s][h * rows : (h + 1) * rows, :] = total[pl.ds(start, rows), sides[c]]


def order_kernel(charge_ref, onto_ref):
    onto_ref[...] = sorter(places_of(charge_ref[...], charge_ref.shape[1] // NQ))


def last_kernel(spot_ref, onto_ref, energy_ref, spread_ref, initial_ref, step_ref, *refs):
    kept, sent, out_ref = refs[:2], refs[2:4], refs[4]
    image = jnp.concatenate([a[...] + b[...] for a, b in zip(kept, sent)], axis=1)
    packed = 2.0 * (image - energy_ref[...] * step_ref[...]) / spread_ref[...] - initial_ref[...]
    block = packed.shape[1]
    spot = jnp.broadcast_to(spot_ref[...][:, :1], packed.shape)
    held = [(spot >= float(q * block)) & (spot < float((q + 1) * block)) for q in range(NQ)]
    high = packed.astype(BF16).astype(F32)
    wide = [
        jnp.concatenate([jnp.where(here, piece, 0.0) for here in held], axis=1) for piece in (high, packed - high)
    ]
    both = mm(jnp.concatenate(wide, axis=0).astype(BF16), onto_ref[...])
    rows = packed.shape[0]
    out_ref[...] = both[:rows, :] + both[rows:, :]


def join_kernel(first_ref, second_ref, out_ref):
    rows = first_ref.shape[0]
    out_ref[:rows, :] = first_ref[...]
    out_ref[rows:, :] = second_ref[...]


def sum_kernel(count, *refs):
    parts, outs = refs[:count], refs[count:]
    rows, width = outs[0].shape
    across = parts[0].shape[1] // width
    for i, out in enumerate(outs):
        here = (slice((i // across) * rows, (i // across + 1) * rows), slice((i % across) * width, (i % across + 1) * width))
        value = parts[0][here]
        for part in parts[1:]:
            value = value + part[here]
        out[...] = value


def choose_kernel(segment_ref, own_ref, shifted_ref, out_ref, held, arrived, left):
    steps = arrived.shape[0]
    rows = own_ref.shape[0] // steps
    parts = [slice(q * rows, (q + 1) * rows) for q in range(steps)]

    @pl.when(segment_ref[0] == 0)
    def _():
        ins = [pltpu.make_async_copy(own_ref.at[p], held.at[p], arrived.at[q]) for q, p in enumerate(parts)]
        outs = [pltpu.make_async_copy(held.at[p], out_ref.at[p], left.at[q]) for q, p in enumerate(parts)]
        for copy in ins:
            copy.start()
        for come, go in zip(ins, outs):
            come.wait()
            go.start()
        for copy in outs:
            copy.wait()

    @pl.when(segment_ref[0] != 0)
    def _():
        copy = pltpu.make_async_copy(shifted_ref, out_ref, left.at[0])
        copy.start()
        copy.wait()


def passed_along(value, axis, steps):
    count = lax.axis_size(axis)
    first, last = (max(0, -steps), min(count, count - steps))
    return lax.ppermute(value, axis, [(source, source + steps) for source in range(first, last)])


def near(value):
    return pltpu.with_memory_space_constraint(value, pltpu.VMEM)


def far(value):
    return pltpu.with_memory_space_constraint(value, pltpu.HBM)


def swapped(value, axis, mask):
    count = lax.axis_size(axis)
    return near(lax.ppermute(value, axis, [(source, source ^ mask) for source in range(count)]))


def call(kernel, ins, outs, scratch, *operands, params=SMALL):
    return pl.pallas_call(
        kernel,
        in_specs=ins,
        out_specs=[VMEM] * len(outs),
        out_shape=outs,
        scratch_shapes=scratch,
        compiler_params=params,
    )(*operands)


def summed(shape, *parts):
    size = parts[0].shape
    outs = [pltpu.VMEM(shape, F32)] * ((size[0] // shape[0]) * (size[1] // shape[1]))
    return call(functools.partial(sum_kernel, len(parts)), [VMEM] * len(parts), outs, [], *parts)


def all_steps(
    left_ops,
    right_ops,
    wavefunction,
    basis_rotation,
    pair_term,
    coupling,
    left_charge,
    right_charge,
):
    own_left = left_ops[0, 0]
    own_right = right_ops[0, 0]
    rows, size = wavefunction.shape[1:]
    block = size // NQ
    count = lax.axis_size("op")
    group = count // 2
    me = jnp.reshape(lax.axis_index("op").astype(jnp.int32), (1,))
    segment = jnp.reshape(lax.axis_index("seg").astype(jnp.int32), (1,))
    me, segment = lax.optimization_barrier((me, segment))

    (packed,) = call(
        pack_kernel,
        [SMEM, HBM, HBM, HBM],
        [pltpu.VMEM((rows, block), F32)],
        [
            pltpu.VMEM((size, LANES), F32),
            pltpu.VMEM((1, size), jnp.int32),
            pltpu.VMEM((1, size), jnp.int32),
            pltpu.VMEM((rows, size), F32),
            pltpu.SemaphoreType.DMA((3,)),
        ],
        me,
        far(left_charge),
        far(right_charge),
        far(wavefunction[0]),
    )
    (pair,) = call(
        join_kernel, [VMEM] * 2, [pltpu.VMEM((2 * rows, block), F32)], [], packed, swapped(packed, "op", group)
    )
    gathered = [pair] + [swapped(pair, "op", s) for s in range(1, group)]

    left_half_high, left_half_low, onto, back, left_column = sort_columns(left_charge, own_left)
    left_high, left_low, right_high, right_low = sort_rest(right_charge, left_half_high, left_half_low, onto, own_right)
    pieces = (left_high, left_low, right_high, right_low)
    halves = [pltpu.VMEM((2 * size, size), BF16), pltpu.VMEM((size, block), F32)]
    pairs = [pltpu.VMEM((2 * rows, block), F32)] * group

    initial, initial_rows, *sent = call(
        functools.partial(first_kernel, group),
        [SMEM, SMEM, SMEM] + [VMEM] * (group + 5),
        [pltpu.VMEM((size, block), F32), pltpu.VMEM((rows, block), F32)] + pairs,
        halves,
        me,
        pair_term,
        coupling,
        onto,
        *gathered,
        *pieces,
        params=LIMIT,
    )
    inner = range(group - 1, 0, -1)
    wings = [pltpu.VMEM((2 * rows, block // 2), F32)] * (2 * group)
    totals = summed((2 * rows, block // 2), sent[0], *[swapped(sent[s], "op", s) for s in inner])
    across = [swapped(total, "op", group) for total in totals]
    gathered = []
    for c in range(2):
        (total,) = summed((2 * rows, block // 2), totals[c], across[c])
        gathered += [total] + [swapped(total, "op", s) for s in inner][::-1]

    energy, spread, step_rows, spot, *sent = call(
        functools.partial(second_kernel, group),
        [SMEM, SMEM, SMEM] + [VMEM] * (2 * group + 7),
        [
            pltpu.VMEM((1, 1), F32),
            pltpu.VMEM((1, 1), F32),
            pltpu.VMEM((rows, block), F32),
            pltpu.VMEM((rows, LANES), F32),
        ]
        + wings,
        halves + [pltpu.VMEM((size, block), F32)],
        me,
        pair_term,
        coupling,
        back,
        near(left_column),
        *gathered,
        initial,
        *pieces,
        params=LIMIT,
    )
    kept, received = [], []
    for c in range(2):
        mine = sent[c * group : (c + 1) * group]
        keep, away = summed((rows, block // 2), near(mine[0]), *[swapped(mine[s], "op", s) for s in inner])
        kept.append(near(keep))
        received.append(swapped(away, "op", group))
    (right_onto,) = call(
        order_kernel, [VMEM], [pltpu.VMEM((size, size), BF16)], [], far(right_charge)
    )
    (chebyshev,) = call(
        last_kernel,
        [VMEM] * 10,
        [jax.ShapeDtypeStruct((rows, size), F32)],
        [],
        near(spot),
        near(right_onto),
        near(energy),
        near(spread),
        near(initial_rows),
        near(step_rows),
        *kept,
        *received,
    )

    turned_left, _ = lax.optimization_barrier((own_left, initial))
    half_turn = jnp.dot(turned_left, basis_rotation[0], precision=lax.Precision.HIGH)
    rotated = lax.dot_general(
        basis_rotation[0], half_turn, (((0,), (0,)), ((), ())), precision=lax.Precision.HIGH
    )
    shifted = passed_along(far(rotated), "seg", 1)
    handed = pl.pallas_call(
        choose_kernel,
        in_specs=[SMEM, HBM, VMEM],
        out_specs=HBM,
        out_shape=jax.ShapeDtypeStruct((size, size), F32),
        scratch_shapes=[
            pltpu.VMEM((size, size), F32),
            pltpu.SemaphoreType.DMA((4 * NQ,)),
            pltpu.SemaphoreType.DMA((4 * NQ,)),
        ],
        compiler_params=SMALL,
    )(segment, far(own_left), near(shifted))[None, None]
    return (chebyshev[None], energy[0], handed)


def solution(mesh):
    placed = (
        P("seg", "op", None, None),
        P("seg", "op", None, None),
        P("seg", "op", None),
        P("seg", None, None),
        P("seg", "op"),
        P(),
        P("seg", None),
        P("seg", None),
    )
    return jax.shard_map(
        all_steps,
        mesh=mesh,
        in_specs=placed,
        out_specs=(P("seg", "op", None), P("seg"), P("seg", "op", None, None)),
        check_vma=False,
    )
```
